32 devices in a mesh: leaf: 4 (over x, core), sub: 8 (over z, y).
Axes of the slice: x: 2, y: 2, z: 4, core: 2. Of those that a mesh axis runs over, the one named last changes fastest.
Arguments:
- points: bfloat16 [131072, 128], P(('leaf', 'sub')), may hold values from -5 to 5
- charges: bfloat16 [131072, 64], P(('leaf', 'sub')), may hold values from -0.796875 to 0.796875
- near_leaves: int32 [256, 12], P(('leaf', 'sub')), may hold values from 0 to 255, as said below
- leaf_interpolant: bfloat16 [256, 512, 256], P(('leaf', 'sub')), may hold values from -0.25 to 0.25
- skel_leaf: int32 [256, 256], P(('leaf', 'sub')), may hold values from 0 to 511, as said below
- interp_mid: bfloat16 [32, 2048, 256], P(('leaf', 'sub')), may hold values from -0.375 to 0.375
- skel_mid: int32 [32, 256], P(('leaf', 'sub')), may hold values from 0 to 2047, as said below
- mid_partners: int32 [32, 4], P(('leaf', 'sub')), may hold values from 0 to 31, as said below
- interp_top: bfloat16 [4, 2048, 256], P('leaf', 'sub'), may hold values from -0.125 to 0.125
- skel_top: int32 [4, 256], P('leaf'), may hold values from 0 to 2047, as said below
Outputs:
- potential: float32 [131072, 64], P(('leaf', 'sub'))
The draws below stay inside these ranges and needn't reach their ends.
Inputs may be any that keep to these rules, and one draw needn't show every extreme that they name: `near_leaves`: row l lists leaf l first, then 12 - 1 other different leaves of the same top node. Over the rows of one device's 8 leaves, at most 2 different leaves of any one other device are named. `skel_leaf`: different indices in a row. `skel_mid`: different indices in a row. `skel_top`: different indices in a row. `mid_partners`: different middle nodes of the same top node, never the node itself.
All inputs are finite; a program needn't handle non-finite values.
Results may differ from the reference program's by a relative error of at most 0.008.
Values may be sent and summed in bfloat16 or wider, within the bound.
No kernel may reach another device: no remote copies, remote signals or barrier semaphores. Data moves between devices by JAX's collectives and lax.ppermute only.
A program may use at most 128 MiB of HBM per device.

```python
import jax
import jax.numpy as jnp
from jax import lax

LEAF = 512
DIM = 128
RHS = 64
SKEL = 256
NEAR = 12
CAP = 2
FARB = 4
LEAF_DEV = 8
LEAVES = 256
NPTS = 131072
N_LEAF = 4
N_SUB = 8


def draw_points(key, part):
    base_key = jax.random.fold_in(key, 606)
    rank_key, value_key = jax.random.split(base_key)
    ranks = jax.random.permutation(rank_key, DIM).astype(jnp.float32)
    profile = (ranks + 1.0) ** (-0.625)
    total = jnp.sum(profile * profile)
    scales = profile * jnp.sqrt(5.6 / total)
    values = jax.random.normal(value_key, (NPTS, DIM), jnp.float32)
    return jnp.clip(values * scales[None, :], -5.0, 5.0).astype(jnp.bfloat16)


def draw_near_leaves(key, part):
    devices = N_LEAF * N_SUB
    peer_count = N_SUB // 2
    remote = peer_count * CAP
    total = remote + LEAF_DEV
    base_key = jax.random.fold_in(key, 101)

    def one_device(device):
        device_key = jax.random.fold_in(base_key, device)
        first_key, second_key, third_key = jax.random.split(device_key, 3)
        group = device // N_SUB
        place_in = device % N_SUB
        shifted = jax.random.permutation(first_key, N_SUB - 1)[:peer_count]
        peers = (place_in + 1 + shifted) % N_SUB
        picked = jax.vmap(lambda sub_key: jax.random.permutation(sub_key, LEAF_DEV)[:CAP])(jax.random.split(second_key, peer_count))
        far_ids = ((group * N_SUB + peers)[:, None] * LEAF_DEV + picked).reshape(-1)
        own_ids = device * LEAF_DEV + jnp.arange(LEAF_DEV, dtype=jnp.int32)
        candidates = jnp.concatenate((far_ids, own_ids)).astype(jnp.int32)

        def one_row(member, row_key):
            order = jax.random.permutation(row_key, total).astype(jnp.int32)
            forced = jnp.concatenate((jnp.arange(remote, dtype=jnp.int32) % LEAF_DEV == member, jnp.zeros((LEAF_DEV,), bool))).astype(jnp.int32)
            itself = jnp.concatenate((jnp.zeros((remote,), bool), jnp.arange(LEAF_DEV, dtype=jnp.int32) == member)).astype(jnp.int32)
            scores = order + forced * (4 * total) - itself * (4 * total)
            chosen = jnp.argsort(-scores)[:NEAR - 1]
            return jnp.concatenate((own_ids[member][None], candidates[chosen]))
        return jax.vmap(one_row)(jnp.arange(LEAF_DEV, dtype=jnp.int32), jax.random.split(third_key, LEAF_DEV))
    return jax.vmap(one_device)(jnp.arange(devices, dtype=jnp.int32)).reshape(devices * LEAF_DEV, NEAR).astype(jnp.int32)


def draw_rows(key, salt, count, limit):
    row_random_keys = jax.random.split(jax.random.fold_in(key, salt), count)
    return jax.vmap(lambda row_key: jax.random.permutation(row_key, limit)[:SKEL])(row_random_keys).astype(jnp.int32)


def draw_skel_leaf(key, part):
    return draw_rows(key, 202, LEAF_DEV * N_LEAF * N_SUB, LEAF)


def draw_skel_mid(key, part):
    return draw_rows(key, 303, N_LEAF * N_SUB, LEAF_DEV * SKEL)


def draw_skel_top(key, part):
    return draw_rows(key, 404, N_LEAF, N_SUB * SKEL)


def draw_mid_partners(key, part):
    devices = N_LEAF * N_SUB
    base_key = jax.random.fold_in(key, 505)

    def one_device(device):
        shifted = jax.random.permutation(jax.random.fold_in(base_key, device), N_SUB - 1)[:FARB]
        return device // N_SUB * N_SUB + (device % N_SUB + 1 + shifted) % N_SUB
    return jax.vmap(one_device)(jnp.arange(devices, dtype=jnp.int32)).astype(jnp.int32)


def shard_levels(rng, extent, cuts, smallest, largest):
    level = 1.0
    for axis_at, parts in cuts:
        heights = jax.random.uniform(jax.random.fold_in(jax.random.fold_in(rng, 6), axis_at), (parts,), jnp.float32, smallest / len(cuts), largest / len(cuts))
        level = level * jnp.repeat(jnp.exp(heights), extent[axis_at] // parts).reshape((-1,) + (1,) * (len(extent) - 1 - axis_at))
    return level


def bell_draw(key, extent, scale, bound, cuts=(), kind=jnp.bfloat16):
    factor_of = shard_levels(key, extent, cuts, -0.22, 0.18) if cuts else 1.0
    drawn = jax.random.normal(key, extent, jnp.float32) * scale * factor_of
    return jnp.minimum(jnp.maximum(drawn, -bound), bound).astype(kind)


def setup_inputs(seed: int = 0) -> dict:
    splits = jax.random.split(jax.random.key(seed), 11)
    return {
        "points": draw_points(jax.random.fold_in(splits[10], 71), 0),
        "charges": bell_draw(splits[1], (NPTS, RHS), 0.1, 0.796875, ((0, 32),)),
        "near_leaves": draw_near_leaves(jax.random.fold_in(splits[10], 71), 0),
        "leaf_interpolant": bell_draw(splits[3], (LEAVES, LEAF, SKEL), LEAF ** -0.5, 0.25, ((0, 32),)),
        "skel_leaf": draw_skel_leaf(jax.random.fold_in(splits[10], 71), 0),
        "interp_mid": bell_draw(splits[5], (N_LEAF * N_SUB, LEAF_DEV * SKEL, SKEL), SKEL ** -0.5, 0.375, ((0, 32),)),
        "skel_mid": draw_skel_mid(jax.random.fold_in(splits[10], 71), 0),
        "mid_partners": draw_mid_partners(jax.random.fold_in(splits[10], 71), 0),
        "interp_top": bell_draw(splits[8], (N_LEAF, N_SUB * SKEL, SKEL), (N_SUB * SKEL) ** -0.5, 0.125, ((0, 4), (1, 8))),
        "skel_top": draw_skel_top(jax.random.fold_in(splits[10], 71), 0),
    }


kernel_rate = 0.25


def kernel_block(target, source):
    products = jnp.einsum("id,kjd->kij", target.astype(jnp.float32), source.astype(jnp.float32))
    target_sq = jnp.sum(jnp.square(target.astype(jnp.float32)), axis=-1)
    source_sq = jnp.sum(jnp.square(source.astype(jnp.float32)), axis=-1)
    distance = target_sq[None, :, None] + source_sq[:, None, :] - 2.0 * products
    return jnp.exp(-kernel_rate * distance).astype(jnp.bfloat16)


def reference(points, charges, near_leaves, leaf_interpolant, skel_leaf, interp_mid, skel_mid, mid_partners, interp_top, skel_top):
    devices = N_LEAF * N_SUB
    leaves = near_leaves.shape[0]
    coords = points.shape[1]
    rhs_count = charges.shape[1]
    leaf_point_coords = points.reshape(leaves, LEAF, coords)
    leaf_source_charges = charges.reshape(leaves, LEAF, rhs_count)

    def near_leaf(leaf_index):
        listed = near_leaves[leaf_index]
        kernel = kernel_block(leaf_point_coords[leaf_index], leaf_point_coords[listed])
        return jnp.einsum("kij,kjr->ir", kernel.astype(jnp.float32), leaf_source_charges[listed].astype(jnp.float32))

    near_sum = lax.map(near_leaf, jnp.arange(leaves, dtype=jnp.int32))
    leaf_upward = jnp.einsum("tmv,tmz->tvz", leaf_interpolant.astype(jnp.float32), leaf_source_charges.astype(jnp.float32)).astype(jnp.bfloat16)
    leaf_skel = jnp.take_along_axis(leaf_point_coords, skel_leaf[:, :, None], axis=1)
    mid_up = jnp.einsum("nqs,nqr->nsr", interp_mid.astype(jnp.float32), leaf_upward.reshape(devices, -1, rhs_count).astype(jnp.float32)).astype(jnp.bfloat16)
    mid_points = jnp.take_along_axis(leaf_skel.reshape(devices, -1, coords), skel_mid[:, :, None], axis=1)

    def mid_node(node):
        listed = mid_partners[node]
        kernel = kernel_block(mid_points[node], mid_points[listed])
        return jnp.einsum("kij,kjr->ir", kernel.astype(jnp.float32), mid_up[listed].astype(jnp.float32))

    mid_sum = lax.map(mid_node, jnp.arange(devices, dtype=jnp.int32))
    top_weight = jnp.einsum("gqs,gqr->gsr", interp_top.astype(jnp.float32), mid_up.reshape(N_LEAF, -1, rhs_count).astype(jnp.float32)).astype(jnp.bfloat16)
    top_points = jnp.take_along_axis(mid_points.reshape(N_LEAF, -1, coords), skel_top[:, :, None], axis=1)

    def top_node(node):
        kernel = kernel_block(top_points[node], top_points)
        keeping = (jnp.arange(N_LEAF, dtype=jnp.int32) != node).astype(jnp.float32)
        return jnp.einsum("kij,kjr,k->ir", kernel.astype(jnp.float32), top_weight.astype(jnp.float32), keeping)

    top_sum = lax.map(top_node, jnp.arange(N_LEAF, dtype=jnp.int32)).astype(jnp.bfloat16)
    spread = jnp.einsum("gqs,gsr->gqr", interp_top.astype(jnp.float32), top_sum.astype(jnp.float32)).reshape(devices, -1, rhs_count)
    mid_total = (mid_sum + spread).astype(jnp.bfloat16)
    leaf_downward = jnp.einsum("nqs,nsr->nqr", interp_mid.astype(jnp.float32), mid_total.astype(jnp.float32)).astype(jnp.bfloat16).reshape(leaves, -1, rhs_count)
    distant_sum = jnp.einsum("xiv,xvq->xiq", leaf_interpolant.astype(jnp.float32), leaf_downward.astype(jnp.float32))
    return (near_sum + distant_sum).reshape(-1, rhs_count)
```

```python
import functools
import math

import jax
import jax.numpy as jnp
from jax import lax
from jax.experimental import pallas as pl
from jax.experimental.pallas import tpu as pltpu
from jax.sharding import PartitionSpec as P

CAP = 2
UNROLL = 4
LANES = 128
kernel_rate = 0.25
LOG2E = math.log2(math.e)
bf16 = jnp.bfloat16
f32 = jnp.float32
i32 = jnp.int32

ROWS_ROWS = (((1,), (1,)), ((), ()))


def dot(a, b):
    return jnp.dot(a, b, preferred_element_type=f32)


def dot_rows(a, b):
    return lax.dot_general(a, b, ROWS_ROWS, preferred_element_type=f32)


def squares(x):
    xf = x.astype(f32)
    sq = xf * xf
    high = sq.astype(bf16)
    low = (sq - high.astype(f32)).astype(bf16)
    return high, low


def source_term(x):
    high, low = squares(x)
    ones = jnp.ones((x.shape[1], LANES), bf16)
    return (dot(high, ones) + dot(low, ones)) * (-kernel_rate * LOG2E)


def target_term(x):
    high, low = squares(x)
    ones = jnp.ones((8, x.shape[1]), bf16)
    return (dot_rows(ones, high) + dot_rows(ones, low)) * (-kernel_rate * LOG2E)


def kernel_tile(source, source_sq, target, target_sq):
    products = dot_rows(source, target)
    columns = []
    for at in range(0, target.shape[0], LANES):
        exponent = products[:, at : at + LANES] * (2.0 * kernel_rate * LOG2E) + (
            source_sq + target_sq[0:1, at : at + LANES]
        )
        columns.append(jnp.exp2(exponent).astype(bf16))
    return jnp.concatenate(columns, axis=1)


def cost(flops, bytes_accessed, transcendentals=0):
    return pl.CostEstimate(
        flops=int(flops), bytes_accessed=int(bytes_accessed), transcendentals=int(transcendentals)
    )


def params():
    return pltpu.CompilerParams(vmem_limit_bytes=56 << 20)


def want_kernel(leaf_dev, group, where, near, chosen, pool):
    base, self_index = where[0], where[1]
    rows, near_count = near.shape
    width = max(LANES, group * leaf_dev)
    local = near[...] - base
    lane = lax.broadcasted_iota(i32, (rows, width), 1)
    member = lax.rem(lane, leaf_dev)
    owner = lax.div(lane, leaf_dev)
    named = jnp.zeros((rows, width), f32)
    for entry in range(near_count):
        named = jnp.maximum(named, (local[:, entry : entry + 1] == lane).astype(f32))
    wanted = jnp.max(named, axis=0, keepdims=True)
    wanted = jnp.where(owner == self_index, 0.0, jnp.broadcast_to(wanted, (rows, width)))
    row_id = lax.broadcasted_iota(i32, (width, width), 0)
    col_id = lax.broadcasted_iota(i32, (width, width), 1)
    before = (lax.div(row_id, leaf_dev) == lax.div(col_id, leaf_dev)) & (row_id < col_id)
    rank = dot(wanted.astype(bf16), before.astype(f32).astype(bf16))
    slot = lax.broadcasted_iota(i32, (rows, width), 0).astype(f32)
    picked = jnp.where((wanted > 0.0) & (rank == slot), member.astype(f32), 0.0)
    owner_row = lax.broadcasted_iota(i32, (group, width), 0)
    owner_of = lax.div(lax.broadcasted_iota(i32, (group, width), 1), leaf_dev)
    belongs = (owner_row == owner_of).astype(f32).astype(bf16)
    chosen[...] = dot_rows(belongs, picked.astype(bf16)).astype(i32)
    place = jnp.zeros((rows, LANES), i32)
    short_lane = lax.broadcasted_iota(i32, (rows, LANES), 1)
    for entry in range(near_count):
        ids = local[:, entry : entry + 1]
        at = jnp.sum(jnp.where(ids == lane, rank, 0.0), axis=1, keepdims=True).astype(i32)
        entry_owner = lax.div(ids, leaf_dev)
        index = jnp.where(
            entry_owner == self_index,
            lax.rem(ids, leaf_dev),
            leaf_dev + entry_owner * CAP + jnp.clip(at, 0, CAP - 1),
        )
        place = jnp.where(short_lane == entry, index, place)
    pool[...] = place


def want(near_leaves, where, leaf_dev, group):
    rows = near_leaves.shape[0]
    return pl.pallas_call(
        functools.partial(want_kernel, leaf_dev, group),
        out_shape=(
            jax.ShapeDtypeStruct((group, rows), i32),
            jax.ShapeDtypeStruct((rows, LANES), i32),
        ),
        grid_spec=pltpu.PrefetchScalarGridSpec(
            num_scalar_prefetch=1,
            grid=(1,),
            in_specs=[pl.BlockSpec(near_leaves.shape, lambda i, w: (0, 0))],
            out_specs=(
                pl.BlockSpec((group, rows), lambda i, w: (0, 0)),
                pl.BlockSpec((rows, LANES), lambda i, w: (0, 0)),
            ),
        ),
        compiler_params=params(),
        cost_estimate=cost(1e6, 1e5),
        name="want",
    )(where, near_leaves)


def pack_kernel(leaf_size, handed, points, charges, *outs):
    group = outs[0].shape[0]
    rhs = charges.shape[0]

    def one(peer, carry):
        for slot, out in enumerate(outs):
            leaf = handed[peer, slot]
            out[peer, :leaf_size, :] = points[leaf]
            for tile in range(leaf_size // LANES):
                at = pl.multiple_of(leaf * leaf_size + tile * LANES, LANES)
                row = leaf_size + tile * rhs
                out[peer, row : row + rhs, :] = charges[:, pl.ds(at, LANES)]
        return carry

    lax.fori_loop(0, group, one, 0)


def pack(handed, points, charges):
    leaf_dev, leaf_size, coords = points.shape
    group = handed.shape[0]
    rows = leaf_size + leaf_size // LANES * charges.shape[0]
    shape = (group, rows, coords)
    return pl.pallas_call(
        functools.partial(pack_kernel, leaf_size),
        out_shape=tuple(jax.ShapeDtypeStruct(shape, bf16) for _ in range(CAP)),
        grid_spec=pltpu.PrefetchScalarGridSpec(
            num_scalar_prefetch=1,
            grid=(1,),
            in_specs=[
                pl.BlockSpec(points.shape, lambda i, h: (0, 0, 0)),
                pl.BlockSpec(charges.shape, lambda i, h: (0, 0)),
            ],
            out_specs=tuple(pl.BlockSpec(shape, lambda i, h: (0, 0, 0)) for _ in range(CAP)),
        ),
        compiler_params=params(),
        cost_estimate=cost(1e5, 8e6),
        name="pack",
    )(handed, points, charges)


def run_pairs(pool, near_count, leaves, keep, tl, sl, prepared, acc):
    points_t, target_sq, points_s, source_sq, charge_of = prepared

    def scan(leaf, count):
        for entry in range(near_count):
            kept, source = keep(pool[leaf, entry])
            tl[count] = leaf
            sl[count] = source
            count = count + kept.astype(i32)
        return count

    count = lax.fori_loop(leaves[0], leaves[1], scan, jnp.int32(0))

    def one(at):
        target, source = tl[at], sl[at]
        tile = kernel_tile(
            points_s(source), source_sq[source], points_t[target], target_sq[target]
        )
        acc[target] += dot(charge_of(source), tile)

    def several(step, carry):
        for k in range(UNROLL):
            one(step * UNROLL + k)
        return carry

    def single(at, carry):
        one(at)
        return carry

    whole = lax.div(count, UNROLL)
    lax.fori_loop(0, whole, several, 0)
    lax.fori_loop(whole * UNROLL, count, single, 0)


def near_local_kernel(near_count, leaves, pool, points, charges, out, tl, sl, ssq, tsq, acc):
    leaf_dev, leaf_size, _ = points.shape

    def prepare(leaf, carry):
        x = points[leaf]
        ssq[leaf] = source_term(x)
        return carry

    def prepare_target(leaf, carry):
        tsq[leaf] = target_term(points[leaf])
        acc[leaf] = jnp.zeros(acc.shape[1:], f32)
        return carry

    lax.fori_loop(0, leaf_dev, prepare, 0)
    lax.fori_loop(leaves[0], leaves[1], prepare_target, 0)

    def charge_of(source):
        at = pl.multiple_of(source * leaf_size, leaf_size)
        return charges[:, pl.ds(at, leaf_size)]

    def keep(index):
        return index < leaf_dev, index

    prepared = (points, tsq, lambda s: points[s], ssq, charge_of)
    run_pairs(pool, near_count, leaves, keep, tl, sl, prepared, acc)
    for leaf in range(*leaves):
        at = (leaf - leaves[0]) * leaf_size
        out[:, at : at + leaf_size] = acc[leaf]


def near_local(pool, near_count, points, charges, leaves):
    leaf_dev, leaf_size, coords = points.shape
    rhs = charges.shape[0]
    span = leaves[1] - leaves[0]
    pairs = span * near_count / 2
    return pl.pallas_call(
        functools.partial(near_local_kernel, near_count, leaves),
        out_shape=jax.ShapeDtypeStruct((rhs, span * leaf_size), f32),
        grid_spec=pltpu.PrefetchScalarGridSpec(
            num_scalar_prefetch=1,
            grid=(1,),
            in_specs=[
                pl.BlockSpec(points.shape, lambda i, p: (0, 0, 0)),
                pl.BlockSpec(charges.shape, lambda i, p: (0, 0)),
            ],
            out_specs=pl.BlockSpec((rhs, span * leaf_size), lambda i, p: (0, 0)),
            scratch_shapes=[
                pltpu.SMEM((leaf_dev * near_count + 1,), i32),
                pltpu.SMEM((leaf_dev * near_count + 1,), i32),
                pltpu.VMEM((leaf_dev, leaf_size, LANES), f32),
                pltpu.VMEM((leaf_dev, 8, leaf_size), f32),
                pltpu.VMEM((leaf_dev, rhs, leaf_size), f32),
            ],
        ),
        compiler_params=params(),
        cost_estimate=cost(
            pairs * 2 * leaf_size * leaf_size * 4 * (coords + rhs), 3e6, pairs * leaf_size * leaf_size
        ),
        name="near_local",
    )(pool, points, charges)


def near_remote_kernel(near_count, slot, parts, pool, points, got, *refs):
    inits, (out, tl, sl, ssq, tsq, qs, acc) = refs[:parts], refs[parts:]
    leaf_dev, leaf_size, _ = points.shape
    group = got.shape[0]
    rhs = out.shape[0]

    def prepare(peer, carry):
        ssq[peer] = source_term(got[peer, :leaf_size, :])
        for tile in range(leaf_size // LANES):
            row = leaf_size + tile * rhs
            qs[peer, :, tile * LANES : (tile + 1) * LANES] = got[peer, row : row + rhs, :]
        return carry

    def prepare_target(leaf, carry):
        tsq[leaf] = target_term(points[leaf])
        acc[leaf] = jnp.zeros(acc.shape[1:], f32)
        return carry

    lax.fori_loop(0, group, prepare, 0)
    lax.fori_loop(0, leaf_dev, prepare_target, 0)

    def keep(index):
        remote = index - leaf_dev
        return (remote >= 0) & (lax.rem(remote, CAP) == slot), lax.div(remote, CAP)

    prepared = (points, tsq, lambda s: got[s, :leaf_size, :], ssq, lambda s: qs[s])
    run_pairs(pool, near_count, (0, leaf_dev), keep, tl, sl, prepared, acc)
    for leaf in range(leaf_dev):
        at = leaf * leaf_size
        total = acc[leaf]
        for init in inits:
            total = total + init[:, at : at + leaf_size]
        out[:, at : at + leaf_size] = total


def near_remote(pool, near_count, points, got, slot, inits):
    leaf_dev, leaf_size, coords = points.shape
    group = got.shape[0]
    rhs = inits[0].shape[0]
    pairs = leaf_dev * near_count / 4
    return pl.pallas_call(
        functools.partial(near_remote_kernel, near_count, slot, len(inits)),
        out_shape=jax.ShapeDtypeStruct((rhs, leaf_dev * leaf_size), f32),
        grid_spec=pltpu.PrefetchScalarGridSpec(
            num_scalar_prefetch=1,
            grid=(1,),
            in_specs=[
                pl.BlockSpec(points.shape, lambda i, p: (0, 0, 0)),
                pl.BlockSpec(got.shape, lambda i, p: (0, 0, 0)),
            ]
            + [pl.BlockSpec(init.shape, lambda i, p: (0, 0)) for init in inits],
            out_specs=pl.BlockSpec((rhs, leaf_dev * leaf_size), lambda i, p: (0, 0)),
            scratch_shapes=[
                pltpu.SMEM((leaf_dev * near_count + 1,), i32),
                pltpu.SMEM((leaf_dev * near_count + 1,), i32),
                pltpu.VMEM((group, leaf_size, LANES), f32),
                pltpu.VMEM((leaf_dev, 8, leaf_size), f32),
                pltpu.VMEM((group, rhs, leaf_size), bf16),
                pltpu.VMEM((leaf_dev, rhs, leaf_size), f32),
            ],
        ),
        compiler_params=params(),
        cost_estimate=cost(
            pairs * 2 * leaf_size * leaf_size * 4 * (coords + rhs), 5e6, pairs * leaf_size * leaf_size
        ),
        name="near_remote",
    )(pool, points, got, *inits)


def store_halves(out, row, value):
    for tile in range(value.shape[1] // LANES):
        out[row : row + value.shape[0], :] = value[:, tile * LANES : (tile + 1) * LANES]
        row += value.shape[0]
    return row


def load_halves(ref, row, rows, width):
    tiles = [ref[row + t * rows : row + (t + 1) * rows, :] for t in range(width // LANES)]
    return jnp.concatenate(tiles, axis=1)


def up_kernel(charges, leaf_interp, interp_mid, interp_top, mid_points, out, total):
    step = pl.program_id(0)

    @pl.when(step == 0)
    def _():
        total[...] = jnp.zeros_like(total)

    leaf_up = dot(charges[...], leaf_interp[0]).astype(bf16)
    total[...] += dot(leaf_up, interp_mid[...])

    @pl.when(step == pl.num_programs(0) - 1)
    def _():
        mid_up = total[...].astype(bf16)
        top = dot(mid_up, interp_top[...])
        high = top.astype(bf16)
        low = (top - high.astype(f32)).astype(bf16)
        skel = mid_points.shape[0]
        out[:skel, :] = mid_points[...]
        row = store_halves(out, skel, mid_up)
        row = store_halves(out, row, high)
        store_halves(out, row, low)


def up(charges, leaf_interp, interp_mid, interp_top, mid_points):
    leaf_dev, leaf_size, skel = leaf_interp.shape
    rhs = charges.shape[0]
    rows = skel + 3 * rhs * (skel // LANES)
    return pl.pallas_call(
        up_kernel,
        out_shape=jax.ShapeDtypeStruct((rows, LANES), bf16),
        grid=(leaf_dev,),
        in_specs=[
            pl.BlockSpec((rhs, leaf_size), lambda i: (0, i)),
            pl.BlockSpec((1, leaf_size, skel), lambda i: (i, 0, 0)),
            pl.BlockSpec((skel, skel), lambda i: (i, 0)),
            pl.BlockSpec(interp_top.shape, lambda i: (0, 0)),
            pl.BlockSpec(mid_points.shape, lambda i: (0, 0)),
        ],
        out_specs=pl.BlockSpec((rows, LANES), lambda i: (0, 0)),
        scratch_shapes=[pltpu.VMEM((rhs, skel), f32)],
        compiler_params=params(),
        cost_estimate=cost(3e8, 4e6),
        name="up",
    )(charges, leaf_interp, interp_mid, interp_top, mid_points)


def far_kernel(partners, mids, tops, interp_top, interp_mid, leaf_interp, out, total):
    step = pl.program_id(0)
    rhs, skel = total.shape

    @pl.when(step == 0)
    def _():
        def pair(source_ref, target, target_sq):
            source = source_ref[:skel, :]
            weight = load_halves(source_ref, skel, rhs, skel)
            tile = kernel_tile(source, source_term(source), target, target_sq)
            return dot(weight, tile)

        target = tops[0, :skel, :]
        target_sq = target_term(target)
        top_sum = jnp.zeros((rhs, skel), f32)
        for other in range(1, tops.shape[0]):
            top_sum = top_sum + pair(tops.at[other], target, target_sq)
        target = mids[0, :skel, :]
        target_sq = target_term(target)
        mid_sum = jnp.zeros((rhs, skel), f32)
        for at in range(partners.shape[0]):
            mid_sum = mid_sum + pair(mids.at[partners[at]], target, target_sq)
        total[...] = (mid_sum + dot_rows(top_sum.astype(bf16), interp_top[...])).astype(bf16)

    leaf_down = dot_rows(total[...], interp_mid[...]).astype(bf16)
    out[...] = dot_rows(leaf_down, leaf_interp[0])


def far(partners, mids, tops, interp_top, interp_mid, leaf_interp):
    leaf_dev, leaf_size, skel = leaf_interp.shape
    rhs = (mids.shape[1] - skel) // (3 * (skel // LANES))
    return pl.pallas_call(
        far_kernel,
        out_shape=jax.ShapeDtypeStruct((rhs, leaf_dev * leaf_size), f32),
        grid_spec=pltpu.PrefetchScalarGridSpec(
            num_scalar_prefetch=1,
            grid=(leaf_dev,),
            in_specs=[
                pl.BlockSpec(mids.shape, lambda i, p: (0, 0, 0)),
                pl.BlockSpec(tops.shape, lambda i, p: (0, 0, 0)),
                pl.BlockSpec(interp_top.shape, lambda i, p: (0, 0)),
                pl.BlockSpec((skel, skel), lambda i, p: (i, 0)),
                pl.BlockSpec((1, leaf_size, skel), lambda i, p: (i, 0, 0)),
            ],
            out_specs=pl.BlockSpec((rhs, leaf_size), lambda i, p: (0, i)),
            scratch_shapes=[pltpu.VMEM((rhs, skel), bf16)],
        ),
        compiler_params=params(),
        cost_estimate=cost(1e9, 6e6, 5e5),
        name="far",
    )(partners, mids, tops, interp_top, interp_mid, leaf_interp)


def share(value, axis, size):
    gathered = value[None]
    bit = size // 2
    while bit:
        swap = [(i, i ^ bit) for i in range(size)]
        other = lax.ppermute(gathered, axis, swap)
        gathered = jnp.stack((gathered, other), axis=1).reshape((-1,) + value.shape)
        bit //= 2
    return gathered


def body(
    points,
    charges,
    near_leaves,
    leaf_interpolant,
    skel_leaf,
    interp_mid,
    skel_mid,
    mid_partners,
    interp_top,
    skel_top,
):
    group = lax.axis_size("sub")
    groups = lax.axis_size("leaf")
    self_index = lax.axis_index("sub")
    leaf_dev, leaf_size, skel = leaf_interpolant.shape
    coords = points.shape[1]
    rhs = charges.shape[1]
    near_count = near_leaves.shape[1]
    group_first = lax.axis_index("leaf") * group
    blocks = points.reshape(leaf_dev, leaf_size, coords)
    charges_t = charges.T

    where = jnp.stack((group_first * leaf_dev, self_index)).astype(i32)
    chosen, pool = want(near_leaves, where, leaf_dev, group)
    handed = lax.all_to_all(chosen, "sub", split_axis=0, concat_axis=0, tiled=True)

    leaf_of = skel_mid[0] // skel
    rows = skel_leaf.reshape(-1)[skel_mid[0]] + leaf_of * leaf_size
    mid_points = points[rows]
    message = up(charges_t, leaf_interpolant, interp_mid[0], interp_top[0], mid_points)

    asked = pack(handed, blocks, charges_t)
    got = [lax.all_to_all(a, "sub", split_axis=0, concat_axis=0, tiled=True) for a in asked]

    half = leaf_dev // 2
    near_parts = [
        near_local(pool, near_count, blocks, charges_t, span)
        for span in ((0, half), (half, leaf_dev))
    ]

    mids = share(message, "sub", group)
    per = rhs * (skel // LANES)
    picked = skel_top[0]
    place = jnp.bitwise_xor(picked // skel, self_index) * mids.shape[1] + picked % skel
    top_points = mids.reshape(-1, LANES)[place]
    parts = mids[:, skel + per :, :].astype(f32)
    top_weight = jnp.sum(parts[:, :per, :] + parts[:, per:, :], axis=0).astype(bf16)
    tops = share(jnp.concatenate((top_points, top_weight), axis=0), "leaf", groups)

    partners = jnp.bitwise_xor(mid_partners[0] - group_first, self_index)
    distant = far(partners, mids, tops, interp_top[0], interp_mid[0], leaf_interpolant)
    near = jnp.concatenate(near_parts, axis=1)
    near = near_remote(pool, near_count, blocks, got[0], 0, (near,))
    return near_remote(pool, near_count, blocks, got[1], 1, (near, distant)).T


def solution(mesh):
    placed = (
        P(("leaf", "sub"), None),
        P(("leaf", "sub"), None),
        P(("leaf", "sub"), None),
        P(("leaf", "sub"), None, None),
        P(("leaf", "sub"), None),
        P(("leaf", "sub"), None, None),
        P(("leaf", "sub"), None),
        P(("leaf", "sub"), None),
        P("leaf", "sub", None),
        P("leaf", None),
    )
    return jax.shard_map(
        body, mesh=mesh, in_specs=placed, out_specs=P(("leaf", "sub"), None), check_vma=False
    )
```

```python
import functools
import math

import jax
import jax.numpy as jnp
from jax import lax
from jax.experimental import pallas as pl
from jax.experimental.pallas import tpu as pltpu
from jax.sharding import PartitionSpec as P


CAP = 2
UNROLL = 4
LANES = 128
kernel_rate = 0.25
LOG2E = math.log2(math.e)
bf16 = jnp.bfloat16
f32 = jnp.float32
i32 = jnp.int32

ROWS_ROWS = (((1,), (1,)), ((), ()))


def dot(a, b):
    return jnp.dot(a, b, preferred_element_type=f32)


def dot_rows(a, b):
    return lax.dot_general(a, b, ROWS_ROWS, preferred_element_type=f32)


def squares(x):
    xf = x.astype(f32)
    sq = xf * xf
    high = sq.astype(bf16)
    low = (sq - high.astype(f32)).astype(bf16)
    return high, low


def source_term(x):
    high, low = squares(x)
    ones = jnp.ones((x.shape[1], LANES), bf16)
    return (dot(high, ones) + dot(low, ones)) * (-kernel_rate * LOG2E)


def target_term(x):
    high, low = squares(x)
    ones = jnp.ones((8, x.shape[1]), bf16)
    return (dot_rows(ones, high) + dot_rows(ones, low)) * (-kernel_rate * LOG2E)


def kernel_tile(source, source_sq, target, target_sq):
    products = dot_rows(source, target)
    columns = []
    for at in range(0, target.shape[0], LANES):
        exponent = products[:, at : at + LANES] * (2.0 * kernel_rate * LOG2E) + (
            source_sq + target_sq[0:1, at : at + LANES]
        )
        columns.append(jnp.exp2(exponent).astype(bf16))
    return jnp.concatenate(columns, axis=1)


def cost(flops, bytes_accessed, transcendentals=0):
    return pl.CostEstimate(
        flops=int(flops), bytes_accessed=int(bytes_accessed), transcendentals=int(transcendentals)
    )


def room(shapes):
    total = 0
    for shape in shapes:
        count = shape.dtype.itemsize * math.prod(shape.shape[:-1])
        total += count * -(-shape.shape[-1] // LANES) * LANES
    return total


def call(kernel, out_shape, in_specs, estimate, operands, scratch=(), own=0):
    outs = out_shape if isinstance(out_shape, (tuple, list)) else [out_shape]
    grant = room(operands) + room(outs) + own + (2 << 20)
    return pl.pallas_call(
        kernel,
        out_shape=out_shape,
        in_specs=in_specs,
        out_specs=[vmem()] * len(outs) if outs is out_shape else vmem(),
        scratch_shapes=list(scratch),
        compiler_params=pltpu.CompilerParams(vmem_limit_bytes=grant),
        cost_estimate=estimate,
    )(*operands)


def vmem():
    return pl.BlockSpec(memory_space=pltpu.VMEM)


def smem():
    return pl.BlockSpec(memory_space=pltpu.SMEM)


def want_kernel(leaf_dev, group, where, near, chosen, pool):
    base, self_index = where[0], where[1]
    rows, near_count = near.shape
    width = max(LANES, group * leaf_dev)
    local = near[...] - base
    lane = lax.broadcasted_iota(i32, (rows, width), 1)
    member = lax.rem(lane, leaf_dev)
    owner = lax.div(lane, leaf_dev)
    named = jnp.zeros((rows, width), f32)
    for entry in range(near_count):
        named = jnp.maximum(named, (local[:, entry : entry + 1] == lane).astype(f32))
    wanted = jnp.max(named, axis=0, keepdims=True)
    wanted = jnp.where(owner == self_index, 0.0, jnp.broadcast_to(wanted, (rows, width)))
    row_id = lax.broadcasted_iota(i32, (width, width), 0)
    col_id = lax.broadcasted_iota(i32, (width, width), 1)
    before = (lax.div(row_id, leaf_dev) == lax.div(col_id, leaf_dev)) & (row_id < col_id)
    rank = dot(wanted.astype(bf16), before.astype(f32).astype(bf16))
    slot = lax.broadcasted_iota(i32, (rows, width), 0).astype(f32)
    picked = jnp.where((wanted > 0.0) & (rank == slot), member.astype(f32), 0.0)
    owner_row = lax.broadcasted_iota(i32, (group, width), 0)
    owner_of = lax.div(lax.broadcasted_iota(i32, (group, width), 1), leaf_dev)
    belongs = (owner_row == owner_of).astype(f32).astype(bf16)
    chosen[...] = dot_rows(belongs, picked.astype(bf16)).astype(i32)
    place = jnp.zeros((rows, LANES), i32)
    short_lane = lax.broadcasted_iota(i32, (rows, LANES), 1)
    for entry in range(near_count):
        ids = local[:, entry : entry + 1]
        at = jnp.sum(jnp.where(ids == lane, rank, 0.0), axis=1, keepdims=True).astype(i32)
        distance = jnp.bitwise_xor(lax.div(ids, leaf_dev), self_index)
        index = jnp.where(
            distance == 0,
            lax.rem(ids, leaf_dev),
            leaf_dev + distance * CAP + jnp.clip(at, 0, CAP - 1),
        )
        place = jnp.where(short_lane == entry, index, place)
    pool[...] = place


def want(near_leaves, where, leaf_dev, group):
    rows = near_leaves.shape[0]
    return call(
        functools.partial(want_kernel, leaf_dev, group),
        [jax.ShapeDtypeStruct((group, rows), i32), jax.ShapeDtypeStruct((rows, LANES), i32)],
        [smem(), vmem()],
        cost(1e6, 1e5),
        (where, near_leaves),
    )


def pack_kernel(leaf_size, where, handed, points, charges, *outs):
    self_index = where[1]
    rhs = charges.shape[0]
    for at, out in enumerate(outs):
        peer = jnp.bitwise_xor(self_index, at + 1)
        for slot in range(CAP):
            leaf = handed[peer, slot]
            out[slot, :leaf_size, :] = points[leaf]
            for tile in range(leaf_size // LANES):
                lane = pl.multiple_of(leaf * leaf_size + tile * LANES, LANES)
                row = leaf_size + tile * rhs
                out[slot, row : row + rhs, :] = charges[:, pl.ds(lane, LANES)]


def pack(where, handed, points, charges):
    _, leaf_size, coords = points.shape
    group = handed.shape[0]
    rows = leaf_size + leaf_size // LANES * charges.shape[0]
    return call(
        functools.partial(pack_kernel, leaf_size),
        [jax.ShapeDtypeStruct((CAP, rows, coords), bf16) for _ in range(group - 1)],
        [smem(), smem(), vmem(), vmem()],
        cost(1e5, 8e6),
        (where, handed, points, charges),
    )


def run_pairs(pool, near_count, leaves, keep, tl, sl, tile_of, charge_of, acc):
    def scan(leaf, count):
        for entry in range(near_count):
            kept, source = keep(pool[leaf, entry])
            tl[count] = leaf
            sl[count] = source
            count = count + kept.astype(i32)
        return count

    count = lax.fori_loop(leaves[0], leaves[1], scan, jnp.int32(0))

    def one(at):
        target, source = tl[at], sl[at]
        acc[target] += dot(charge_of(source), tile_of(target, source))

    def several(step, carry):
        for k in range(UNROLL):
            one(step * UNROLL + k)
        return carry

    def single(at, carry):
        one(at)
        return carry

    whole = lax.div(count, UNROLL)
    lax.fori_loop(0, whole, several, 0)
    lax.fori_loop(whole * UNROLL, count, single, 0)


def near_cost(pairs, leaf_size, coords, rhs):
    return cost(
        pairs * 2 * leaf_size * leaf_size * 4 * (coords + rhs), 3e6, pairs * leaf_size * leaf_size
    )


def near_local_kernel(near_count, leaves, pool, points, charges, *refs):
    if leaves[0] == 0:
        out, tsq, tl, sl, ssq, acc = refs
    else:
        tsq, out, tl, sl, ssq, acc = refs
    leaf_dev, leaf_size, _ = points.shape

    def prepare(leaf, carry):
        ssq[leaf] = source_term(points[leaf])
        if leaves[0] == 0:
            tsq[leaf] = target_term(points[leaf])
        return carry

    lax.fori_loop(0, leaf_dev, prepare, 0)
    for leaf in range(*leaves):
        acc[leaf] = jnp.zeros(acc.shape[1:], f32)

    def charge_of(source):
        at = pl.multiple_of(source * leaf_size, leaf_size)
        return charges[:, pl.ds(at, leaf_size)]

    def tile_of(target, source):
        return kernel_tile(points[source], ssq[source], points[target], tsq[target])

    def keep(index):
        return index < leaf_dev, index

    run_pairs(pool, near_count, leaves, keep, tl, sl, tile_of, charge_of, acc)
    for leaf in range(*leaves):
        at = (leaf - leaves[0]) * leaf_size
        out[:, at : at + leaf_size] = acc[leaf]


def near_local(pool, near_count, points, charges, leaves, *tsq):
    leaf_dev, leaf_size, coords = points.shape
    rhs = charges.shape[0]
    span = leaves[1] - leaves[0]
    result = jax.ShapeDtypeStruct((rhs, span * leaf_size), f32)
    terms = jax.ShapeDtypeStruct((leaf_dev, 8, leaf_size), f32)
    return call(
        functools.partial(near_local_kernel, near_count, leaves),
        result if tsq else [result, terms],
        [smem(), vmem(), vmem()] + [vmem()] * len(tsq),
        near_cost(span * near_count / 2, leaf_size, coords, rhs),
        (pool, points, charges) + tsq,
        scratch=[
            pltpu.SMEM((leaf_dev * near_count + 1,), i32),
            pltpu.SMEM((leaf_dev * near_count + 1,), i32),
            pltpu.VMEM((leaf_dev, leaf_size, LANES), f32),
            pltpu.VMEM((leaf_dev, rhs, leaf_size), f32),
        ],
        own=leaf_dev * leaf_size * (rhs + LANES) * 4 + (1 << 20),
    )


def near_remote_kernel(near_count, first, parts, extra, pool, points, tsq, *refs):
    got, inits, refs = refs[:parts], refs[parts : parts + extra], refs[parts + extra :]
    out, tl, sl, pts, ssq, qs, acc = refs
    leaf_dev, leaf_size, _ = points.shape
    rhs = out.shape[0]

    for part, message in enumerate(got):
        def prepare(slot, carry, part=part, message=message):
            place = part * CAP + slot
            x = message[slot, :leaf_size, :]
            pts[place] = x
            ssq[place] = source_term(x)
            for tile in range(leaf_size // LANES):
                row = leaf_size + tile * rhs
                qs[place, :, tile * LANES : (tile + 1) * LANES] = message[slot, row : row + rhs, :]
            return carry

        lax.fori_loop(0, CAP, prepare, 0)

    width = 0
    for init in inits:
        span = init.shape[1] // leaf_size
        for leaf in range(span):
            value = init[:, leaf * leaf_size : (leaf + 1) * leaf_size]
            target = (width + leaf) % leaf_dev
            if width + leaf < leaf_dev:
                acc[target] = value
            else:
                acc[target] += value
        width += span

    low = leaf_dev + first * CAP

    def keep(index):
        return (index >= low) & (index < low + parts * CAP), index - low

    def tile_of(target, source):
        return kernel_tile(pts[source], ssq[source], points[target], tsq[target])

    run_pairs(
        pool, near_count, (0, leaf_dev), keep, tl, sl, tile_of, lambda s: qs[s], acc
    )
    for leaf in range(leaf_dev):
        out[:, leaf * leaf_size : (leaf + 1) * leaf_size] = acc[leaf]


def near_remote(pool, near_count, points, tsq, first, got, inits):
    leaf_dev, leaf_size, coords = points.shape
    rhs = inits[0].shape[0]
    places = len(got) * CAP
    return call(
        functools.partial(near_remote_kernel, near_count, first, len(got), len(inits)),
        jax.ShapeDtypeStruct((rhs, leaf_dev * leaf_size), f32),
        [smem(), vmem(), vmem()] + [vmem()] * (len(got) + len(inits)),
        near_cost(len(got) * leaf_dev, leaf_size, coords, rhs),
        (pool, points, tsq, *got, *inits),
        scratch=[
            pltpu.SMEM((leaf_dev * near_count + 1,), i32),
            pltpu.SMEM((leaf_dev * near_count + 1,), i32),
            pltpu.VMEM((places, leaf_size, coords), bf16),
            pltpu.VMEM((places, leaf_size, LANES), f32),
            pltpu.VMEM((places, rhs, leaf_size), bf16),
            pltpu.VMEM((leaf_dev, rhs, leaf_size), f32),
        ],
        own=(leaf_dev * rhs * 4 + places * (coords * 2 + LANES * 4 + rhs * 2)) * leaf_size
        + (2 << 20),
    )


def store_halves(out, row, value):
    for tile in range(value.shape[1] // LANES):
        out[row : row + value.shape[0], :] = value[:, tile * LANES : (tile + 1) * LANES]
        row += value.shape[0]
    return row


def load_halves(ref, row, rows, width):
    tiles = [ref[row + t * rows : row + (t + 1) * rows, :] for t in range(width // LANES)]
    return jnp.concatenate(tiles, axis=1)


def up_kernel(charges, leaf_interp, interp_mid, interp_top, mid_points, out):
    leaf_dev, leaf_size, skel = leaf_interp.shape
    total = jnp.zeros((charges.shape[0], skel), f32)
    for leaf in range(leaf_dev):
        block = charges[:, leaf * leaf_size : (leaf + 1) * leaf_size]
        leaf_up = dot(block, leaf_interp[leaf]).astype(bf16)
        total = total + dot(leaf_up, interp_mid[leaf * skel : (leaf + 1) * skel, :])
    mid_up = total.astype(bf16)
    top = dot(mid_up, interp_top[...])
    out[:skel, :] = mid_points[...]
    row = store_halves(out, skel, mid_up)
    store_halves(out, row, top.astype(bf16))


def up(charges, leaf_interp, interp_mid, interp_top, mid_points):
    _, _, skel = leaf_interp.shape
    rhs = charges.shape[0]
    rows = skel + 2 * rhs * (skel // LANES)
    return call(
        up_kernel,
        jax.ShapeDtypeStruct((rows, LANES), bf16),
        [vmem()] * 5,
        cost(3e8, 4e6),
        (charges, leaf_interp, interp_mid, interp_top, mid_points),
    )


def far_kernel(partners, mids, tops, interp_top, interp_mid, leaf_interp, out):
    leaf_dev, leaf_size, skel = leaf_interp.shape
    rhs = out.shape[0]

    def pair(source_ref, target, target_sq):
        source = source_ref[:skel, :]
        weight = load_halves(source_ref, skel, rhs, skel)
        tile = kernel_tile(source, source_term(source), target, target_sq)
        return dot(weight, tile)

    target = tops[0, :skel, :]
    target_sq = target_term(target)
    top_sum = jnp.zeros((rhs, skel), f32)
    for other in range(1, tops.shape[0]):
        top_sum = top_sum + pair(tops.at[other], target, target_sq)
    target = mids[0, :skel, :]
    target_sq = target_term(target)
    mid_sum = jnp.zeros((rhs, skel), f32)
    for at in range(partners.shape[0]):
        mid_sum = mid_sum + pair(mids.at[partners[at]], target, target_sq)
    total = (mid_sum + dot_rows(top_sum.astype(bf16), interp_top[...])).astype(bf16)
    for leaf in range(leaf_dev):
        block = interp_mid[leaf * skel : (leaf + 1) * skel, :]
        leaf_down = dot_rows(total, block).astype(bf16)
        out[:, leaf * leaf_size : (leaf + 1) * leaf_size] = dot_rows(leaf_down, leaf_interp[leaf])


def far(partners, mids, tops, interp_top, interp_mid, leaf_interp):
    leaf_dev, leaf_size, skel = leaf_interp.shape
    rhs = (mids.shape[1] - skel) // (2 * (skel // LANES))
    return call(
        far_kernel,
        jax.ShapeDtypeStruct((rhs, leaf_dev * leaf_size), f32),
        [smem()] + [vmem()] * 5,
        cost(1e9, 6e6, 5e5),
        (partners, mids, tops, interp_top, interp_mid, leaf_interp),
        own=1 << 20,
    )


def swapped(value, axis, size, distance):
    return lax.ppermute(value, axis, [(i, i ^ distance) for i in range(size)])


def share_halves(value, axis, size):
    half = size // 2
    pair = jnp.stack((value, swapped(value, axis, size, half)))
    others = [swapped(pair, axis, size, d) for d in range(1, half)]
    return jnp.concatenate([pair] + others, axis=0)


def place(distance, size):
    half = size // 2
    return distance % half * 2 + distance // half


def share(value, axis, size):
    gathered = value[None]
    while gathered.shape[0] < size:
        at = gathered.shape[0]
        other = swapped(gathered, axis, size, at)
        gathered = jnp.concatenate((gathered, other), axis=0)
    return gathered


def near_spans(group):
    half = group // 2
    spans = [(half, half + half // 2), (1, half)]
    spans += [(half + half // 2, half + half * 3 // 4), (half + half * 3 // 4, group)]
    return [span for span in spans if span[1] > span[0]]


def body(
    points,
    charges,
    near_leaves,
    leaf_interpolant,
    skel_leaf,
    interp_mid,
    skel_mid,
    mid_partners,
    interp_top,
    skel_top,
):
    group = lax.axis_size("sub")
    groups = lax.axis_size("leaf")
    self_index = lax.axis_index("sub")
    leaf_dev, leaf_size, skel = leaf_interpolant.shape
    coords = points.shape[1]
    rhs = charges.shape[1]
    near_count = near_leaves.shape[1]
    group_first = lax.axis_index("leaf") * group
    blocks = points.reshape(leaf_dev, leaf_size, coords)
    charges_t = charges.T

    where = jnp.stack((group_first * leaf_dev, self_index)).astype(i32)
    chosen, pool = want(near_leaves, where, leaf_dev, group)
    handed = lax.all_to_all(chosen, "sub", split_axis=0, concat_axis=0, tiled=True)

    leaf_of = skel_mid[0] // skel
    rows = skel_leaf.reshape(-1)[skel_mid[0]] + leaf_of * leaf_size
    mid_points = points[rows]
    message = up(charges_t, leaf_interpolant, interp_mid[0], interp_top[0], mid_points)

    asked = pack(where, handed, blocks, charges_t)
    got = []
    for distance, one in enumerate(asked, 1):
        got.append(swapped(one, "sub", group, distance))

    half = leaf_dev // 2
    first, tsq = near_local(pool, near_count, blocks, charges_t, (0, half))
    second = near_local(pool, near_count, blocks, charges_t, (half, leaf_dev), tsq)
    sums = [first, second]

    mids = share_halves(message, "sub", group)
    per = rhs * (skel // LANES)
    picked = skel_top[0]
    node = place(jnp.bitwise_xor(picked // skel, self_index), group)
    top_points = mids.reshape(-1, LANES)[node * mids.shape[1] + picked % skel]
    top_weight = jnp.sum(mids[:, skel + per :, :].astype(f32), axis=0).astype(bf16)
    tops = share(jnp.concatenate((top_points, top_weight), axis=0), "leaf", groups)

    partners = place(jnp.bitwise_xor(mid_partners[0] - group_first, self_index), group)
    distant = far(partners, mids, tops, interp_top[0], interp_mid[0], leaf_interpolant)
    spans = near_spans(group)
    for at, span in enumerate(spans):
        if at == len(spans) - 1:
            sums.append(distant)
        part = got[span[0] - 1 : span[1] - 1]
        sums = [near_remote(pool, near_count, blocks, tsq, span[0], part, sums)]
    return sums[0].T


def solution(mesh):
    placed = (
        P(("leaf", "sub"), None),
        P(("leaf", "sub"), None),
        P(("leaf", "sub"), None),
        P(("leaf", "sub"), None, None),
        P(("leaf", "sub"), None),
        P(("leaf", "sub"), None, None),
        P(("leaf", "sub"), None),
        P(("leaf", "sub"), None),
        P("leaf", "sub", None),
        P("leaf", None),
    )
    return jax.shard_map(
        body, mesh=mesh, in_specs=placed, out_specs=P(("leaf", "sub"), None), check_vma=False
    )
```

```python
import functools
import math

import jax
import jax.numpy as jnp
from jax import lax
from jax.experimental import pallas as pl
from jax.experimental.pallas import tpu as pltpu
from jax.sharding import PartitionSpec as P


CAP = 2
UNROLL = 4
LANES = 128
kernel_rate = 0.25
VMEM_BYTES = 67043328
LOG2E = math.log2(math.e)
bf16 = jnp.bfloat16
f32 = jnp.float32
i32 = jnp.int32

ROWS_ROWS = (((1,), (1,)), ((), ()))


def dot(a, b):
    return jnp.dot(a, b, preferred_element_type=f32)


def dot_rows(a, b):
    return lax.dot_general(a, b, ROWS_ROWS, preferred_element_type=f32)


def squares(x):
    xf = x.astype(f32)
    sq = xf * xf
    high = sq.astype(bf16)
    low = (sq - high.astype(f32)).astype(bf16)
    return high, low


def source_term(x):
    high, low = squares(x)
    ones = jnp.ones((x.shape[1], LANES), bf16)
    return (dot(high, ones) + dot(low, ones)) * (-kernel_rate * LOG2E)


def target_term(x):
    high, low = squares(x)
    ones = jnp.ones((8, x.shape[1]), bf16)
    return (dot_rows(ones, high) + dot_rows(ones, low)) * (-kernel_rate * LOG2E)


def kernel_tile(source, source_sq, target, target_sq):
    products = dot_rows(source, target)
    columns = []
    for at in range(0, target.shape[0], LANES):
        exponent = products[:, at : at + LANES] * (2.0 * kernel_rate * LOG2E) + (
            source_sq + target_sq[0:1, at : at + LANES]
        )
        columns.append(jnp.exp2(exponent).astype(bf16))
    return jnp.concatenate(columns, axis=1)


def cost(flops, bytes_accessed, transcendentals=0):
    return pl.CostEstimate(
        flops=int(flops), bytes_accessed=int(bytes_accessed), transcendentals=int(transcendentals)
    )


def room(shapes):
    total = 0
    for shape in shapes:
        count = shape.dtype.itemsize * math.prod(shape.shape[:-1])
        total += count * -(-shape.shape[-1] // LANES) * LANES
    return total


def in_hbm():
    return pl.BlockSpec(memory_space=pltpu.HBM)


def copy_in(source, target, sem):
    made = pltpu.make_async_copy(source, target, sem)
    made.start()
    return made


def call(kernel, out_shape, in_specs, estimate, operands, scratch=(), own=0, outs=None, alias=None):
    several = isinstance(out_shape, (tuple, list))
    shapes = out_shape if several else [out_shape]
    specs = outs or [vmem()] * len(shapes)
    grant = room(operands) + room(shapes) + own + (2 << 20) if own is not None else VMEM_BYTES
    return pl.pallas_call(
        kernel,
        out_shape=out_shape,
        in_specs=in_specs,
        out_specs=specs if several else specs[0],
        scratch_shapes=list(scratch),
        input_output_aliases=alias or {},
        compiler_params=pltpu.CompilerParams(vmem_limit_bytes=grant),
        cost_estimate=estimate,
    )(*operands)


def vmem():
    return pl.BlockSpec(memory_space=pltpu.VMEM)


def smem():
    return pl.BlockSpec(memory_space=pltpu.SMEM)


def want_kernel(leaf_dev, group, where, near, chosen, pool):
    base, self_index = where[0], where[1]
    rows, near_count = near.shape
    width = max(LANES, group * leaf_dev)
    local = near[...] - base
    lane = lax.broadcasted_iota(i32, (rows, width), 1)
    member = lax.rem(lane, leaf_dev)
    owner = lax.div(lane, leaf_dev)
    named = jnp.zeros((rows, width), f32)
    for entry in range(near_count):
        named = jnp.maximum(named, (local[:, entry : entry + 1] == lane).astype(f32))
    wanted = jnp.max(named, axis=0, keepdims=True)
    wanted = jnp.where(owner == self_index, 0.0, jnp.broadcast_to(wanted, (rows, width)))
    row_id = lax.broadcasted_iota(i32, (width, width), 0)
    col_id = lax.broadcasted_iota(i32, (width, width), 1)
    before = (lax.div(row_id, leaf_dev) == lax.div(col_id, leaf_dev)) & (row_id < col_id)
    rank = dot(wanted.astype(bf16), before.astype(f32).astype(bf16))
    slot = lax.broadcasted_iota(i32, (rows, width), 0).astype(f32)
    picked = jnp.where((wanted > 0.0) & (rank == slot), member.astype(f32), 0.0)
    owner_row = lax.broadcasted_iota(i32, (group, width), 0)
    owner_of = lax.div(lax.broadcasted_iota(i32, (group, width), 1), leaf_dev)
    belongs = (owner_row == owner_of).astype(f32).astype(bf16)
    chosen[...] = dot_rows(belongs, picked.astype(bf16)).astype(i32)
    place = jnp.zeros((rows, LANES), i32)
    short_lane = lax.broadcasted_iota(i32, (rows, LANES), 1)
    for entry in range(near_count):
        ids = local[:, entry : entry + 1]
        at = jnp.sum(jnp.where(ids == lane, rank, 0.0), axis=1, keepdims=True).astype(i32)
        distance = jnp.bitwise_xor(lax.div(ids, leaf_dev), self_index)
        index = jnp.where(
            distance == 0,
            lax.rem(ids, leaf_dev),
            leaf_dev + distance * CAP + jnp.clip(at, 0, CAP - 1),
        )
        place = jnp.where(short_lane == entry, index, place)
    pool[...] = place


def want(near_leaves, where, leaf_dev, group):
    rows = near_leaves.shape[0]
    return call(
        functools.partial(want_kernel, leaf_dev, group),
        [jax.ShapeDtypeStruct((group, rows), i32), jax.ShapeDtypeStruct((rows, LANES), i32)],
        [smem(), vmem()],
        cost(1e6, 1e5),
        (where, near_leaves),
        own=None,
    )


def pack_kernel(leaf_size, distances, where, handed, points, charges, *refs):
    outs, (x, q, sem_x, sem_q, sem_out) = refs[: len(distances)], refs[len(distances) :]
    self_index = where[1]
    rhs = charges.shape[0]
    taken, given = [], []
    for at, distance in enumerate(distances):
        peer = jnp.bitwise_xor(self_index, distance)
        for slot in range(CAP):
            leaf = handed[peer, slot]
            lanes = pl.ds(pl.multiple_of(leaf * leaf_size, leaf_size), leaf_size)
            put = at * CAP + slot
            taken.append(
                (
                    copy_in(points.at[leaf], x.at[put], sem_x.at[put]),
                    copy_in(charges.at[:, lanes], q.at[put], sem_q.at[put]),
                )
            )
    for at, out in enumerate(outs):
        for slot in range(CAP):
            put = at * CAP + slot
            taken[put][0].wait()
            given.append(copy_in(x.at[put], out.at[slot, :leaf_size, :], sem_out.at[put, 0]))
            taken[put][1].wait()
            for tile in range(leaf_size // LANES):
                rows = pl.ds(leaf_size + tile * rhs, rhs)
                lanes = pl.ds(tile * LANES, LANES)
                given.append(
                    copy_in(
                        q.at[put, :, lanes], out.at[slot, rows, :], sem_out.at[put, 1 + tile]
                    )
                )
    for one in given:
        one.wait()


def pack(where, handed, points, charges, distances):
    _, leaf_size, coords = points.shape
    rhs = charges.shape[0]
    rows = leaf_size + leaf_size // LANES * rhs
    places = len(distances) * CAP
    sem = pltpu.SemaphoreType.DMA
    return call(
        functools.partial(pack_kernel, leaf_size, distances),
        [jax.ShapeDtypeStruct((CAP, rows, coords), bf16) for _ in distances],
        [smem(), smem(), in_hbm(), in_hbm()],
        cost(1e5, 2 * places * rows * coords * 2),
        (where, handed, points, charges),
        scratch=[
            pltpu.VMEM((places, leaf_size, coords), bf16),
            pltpu.VMEM((places, rhs, leaf_size), bf16),
            sem((places,)),
            sem((places,)),
            sem((places, 1 + leaf_size // LANES)),
        ],
        own=None,
        outs=[in_hbm()] * len(distances),
    )


def run_pairs(pool, near_count, leaves, keep, tl, sl, tile_of, charge_of, acc, base):
    def scan(leaf, count):
        for entry in range(near_count):
            kept, source = keep(pool[leaf, entry])
            tl[count] = leaf
            sl[count] = source
            count = count + kept.astype(i32)
        return count

    count = lax.fori_loop(leaves[0], leaves[1], scan, jnp.int32(0))

    def one(at):
        target, source = tl[at], sl[at]
        acc[target - base] += dot(charge_of(source), tile_of(target, source))

    def several(step, carry):
        for k in range(UNROLL):
            one(step * UNROLL + k)
        return carry

    def single(at, carry):
        one(at)
        return carry

    whole = lax.div(count, UNROLL)
    lax.fori_loop(0, whole, several, 0)
    lax.fori_loop(whole * UNROLL, count, single, 0)


def near_cost(pairs, leaf_size, coords, rhs):
    return cost(
        pairs * 2 * leaf_size * leaf_size * 4 * (coords + rhs), 3e6, pairs * leaf_size * leaf_size
    )


def near_local_kernel(near_count, leaves, pool, points, charges, *refs):
    if leaves[0] == 0:
        out, tsq, tl, sl, x, q, ssq, acc, sem_x, sem_q, sem_out = refs
    else:
        tsq, out, tl, sl, x, q, ssq, acc, sem_x, sem_q, sem_out = refs
    leaf_dev, leaf_size, _ = points.shape
    q_copy = copy_in(charges, q, sem_q)
    x_copies = [copy_in(points.at[m], x.at[m], sem_x.at[m]) for m in range(leaf_dev)]
    acc[...] = jnp.zeros_like(acc)
    for leaf, waited in enumerate(x_copies):
        waited.wait()
        ssq[leaf] = source_term(x[leaf])
        if leaves[0] == 0:
            tsq[leaf] = target_term(x[leaf])
    q_copy.wait()

    def charge_of(source):
        at = pl.multiple_of(source * leaf_size, leaf_size)
        return q[:, pl.ds(at, leaf_size)]

    def tile_of(target, source):
        return kernel_tile(x[source], ssq[source], x[target], tsq[target])

    def keep(index):
        return index < leaf_dev, index

    run_pairs(pool, near_count, leaves, keep, tl, sl, tile_of, charge_of, acc, leaves[0])
    copy_in(acc, out, sem_out).wait()


def near_local(pool, near_count, points, charges, leaves, *tsq):
    leaf_dev, leaf_size, coords = points.shape
    rhs = charges.shape[0]
    span = leaves[1] - leaves[0]
    result = jax.ShapeDtypeStruct((span, rhs, leaf_size), f32)
    terms = jax.ShapeDtypeStruct((leaf_dev, 8, leaf_size), f32)
    return call(
        functools.partial(near_local_kernel, near_count, leaves),
        result if tsq else [result, terms],
        [smem(), in_hbm(), in_hbm()] + [vmem()] * len(tsq),
        near_cost(span * near_count / 2, leaf_size, coords, rhs),
        (pool, points, charges) + tsq,
        scratch=[
            pltpu.SMEM((leaf_dev * near_count + 1,), i32),
            pltpu.SMEM((leaf_dev * near_count + 1,), i32),
            pltpu.VMEM(points.shape, bf16),
            pltpu.VMEM(charges.shape, bf16),
            pltpu.VMEM((leaf_dev, leaf_size, LANES), f32),
            pltpu.VMEM((span, rhs, leaf_size), f32),
            pltpu.SemaphoreType.DMA((leaf_dev,)),
            pltpu.SemaphoreType.DMA,
            pltpu.SemaphoreType.DMA,
        ],
        own=None,
        outs=[in_hbm()] if tsq else [in_hbm(), vmem()],
    )


def near_remote_kernel(near_count, first, parts, stage, pool, points, tsq, *refs):
    got, refs = refs[:parts], refs[parts:]
    taken = {"first": 2, "middle": 1, "last": 2}[stage]
    inits, refs = refs[:taken], refs[taken:]
    out, tl, sl, x, pts, ssq, qs = refs[:7]
    sem_got, sem_x, sem_acc = refs[-3:]
    acc = refs[7] if stage == "last" else out
    leaf_dev, leaf_size, _ = points.shape
    rhs = acc.shape[1]
    tiles = leaf_size // LANES

    moves = []
    for part, message in enumerate(got):
        for slot in range(CAP):
            at = part * CAP + slot
            one = [copy_in(message.at[slot, :leaf_size, :], pts.at[at], sem_got.at[at, 0])]
            for tile in range(tiles):
                rows = pl.ds(leaf_size + tile * rhs, rhs)
                lanes = pl.ds(tile * LANES, LANES)
                one.append(
                    copy_in(
                        message.at[slot, rows, :], qs.at[at, :, lanes], sem_got.at[at, 1 + tile]
                    )
                )
            moves.append(one)
    x_copy = copy_in(points, x, sem_x)
    acc_copies = []
    if stage == "first":
        base = 0
        for at, init in enumerate(inits):
            rows = pl.ds(base, init.shape[0])
            acc_copies.append(copy_in(init, acc.at[rows], sem_acc.at[at]))
            base += init.shape[0]
    if stage == "last":
        for leaf in range(leaf_dev):
            acc[leaf] = inits[0][leaf] + inits[1][leaf]
    for at, one in enumerate(moves):
        one[0].wait()
        ssq[at] = source_term(pts[at])
        for move in one[1:]:
            move.wait()
    x_copy.wait()
    for move in acc_copies:
        move.wait()

    low = leaf_dev + first * CAP

    def keep(index):
        return (index >= low) & (index < low + parts * CAP), index - low

    def tile_of(target, source):
        return kernel_tile(pts[source], ssq[source], x[target], tsq[target])

    run_pairs(pool, near_count, (0, leaf_dev), keep, tl, sl, tile_of, lambda s: qs[s], acc, 0)
    if stage == "last":
        for leaf in range(leaf_dev):
            out[:, leaf * leaf_size : (leaf + 1) * leaf_size] = acc[leaf]


def near_remote(pool, near_count, points, tsq, first, got, inits, stage):
    leaf_dev, leaf_size, coords = points.shape
    rhs = inits[0].shape[1]
    places = len(got) * CAP
    sums = (leaf_dev, rhs, leaf_size)
    last = stage == "last"
    scratch = [
        pltpu.SMEM((leaf_dev * near_count + 1,), i32),
        pltpu.SMEM((leaf_dev * near_count + 1,), i32),
        pltpu.VMEM(points.shape, bf16),
        pltpu.VMEM((places, leaf_size, coords), bf16),
        pltpu.VMEM((places, leaf_size, LANES), f32),
        pltpu.VMEM((places, rhs, leaf_size), bf16),
    ]
    if last:
        scratch.append(pltpu.VMEM(sums, f32))
    scratch += [
        pltpu.SemaphoreType.DMA((places, 1 + leaf_size // LANES)),
        pltpu.SemaphoreType.DMA,
        pltpu.SemaphoreType.DMA((2,)),
    ]
    spec = in_hbm() if stage == "first" else vmem()
    shape = (rhs, leaf_dev * leaf_size) if last else sums
    return call(
        functools.partial(near_remote_kernel, near_count, first, len(got), stage),
        jax.ShapeDtypeStruct(shape, f32),
        [smem(), in_hbm(), vmem()] + [in_hbm()] * len(got) + [spec] * len(inits),
        near_cost(len(got) * leaf_dev, leaf_size, coords, rhs),
        (pool, points, tsq, *got, *inits),
        scratch=scratch,
        own=(leaf_dev * rhs * 4 + places * (coords * 2 + LANES * 4 + rhs * 2)) * leaf_size
        + (2 << 20),
        alias={3 + len(got): 0} if stage == "middle" else None,
    )


def store_halves(out, row, value):
    for tile in range(value.shape[1] // LANES):
        out[row : row + value.shape[0], :] = value[:, tile * LANES : (tile + 1) * LANES]
        row += value.shape[0]
    return row


def load_halves(ref, row, rows, width):
    tiles = [ref[row + t * rows : row + (t + 1) * rows, :] for t in range(width // LANES)]
    return jnp.concatenate(tiles, axis=1)


def skeleton_rows(skel_leaf, skel_mid, leaf_size):
    leaf_dev, skel = skel_leaf.shape
    column = lax.rem(skel_mid, skel)
    leaf = lax.div(skel_mid, skel)
    hit = lax.broadcasted_iota(i32, (skel, skel), 0) == column
    table = jnp.concatenate((lax.div(skel_leaf, 16), lax.rem(skel_leaf, 16)), axis=0)
    found = dot(table.astype(f32).astype(bf16), hit.astype(f32).astype(bf16))
    index = (found[:leaf_dev] * 16.0 + found[leaf_dev:]).astype(i32)
    row = lax.broadcasted_iota(i32, (leaf_dev, skel), 0)
    return jnp.sum(jnp.where(row == leaf, index + row * leaf_size, 0), axis=0, keepdims=True)


def up_kernel(*refs):
    points, charges, leaf_interp, interp_mid, interp_top, skel_leaf, skel_mid, out = refs[:8]
    x, q, leaf_w, mid_w, top_w, sem_x, sem_l, sem_m, sem_q, sem_t = refs[8:]
    leaf_dev, leaf_size, skel = leaf_interp.shape
    leaves = range(leaf_dev)
    x_copies = [copy_in(points.at[m], x.at[m], sem_x.at[m]) for m in leaves]
    q_copy = copy_in(charges, q, sem_q)
    l_copies, m_copies = [], []
    for m in leaves:
        rows = pl.ds(m * skel, skel)
        l_copies.append(copy_in(leaf_interp.at[m], leaf_w.at[m], sem_l.at[m]))
        m_copies.append(copy_in(interp_mid.at[rows], mid_w.at[rows], sem_m.at[m]))
    t_copy = copy_in(interp_top, top_w, sem_t)

    rows = skeleton_rows(skel_leaf[...], skel_mid[...], leaf_size)
    at = lax.broadcasted_iota(i32, (leaf_size, skel), 0)
    columns = (((0,), (0,)), ((), ()))
    picked = jnp.zeros((skel, x.shape[2]), f32)
    for m in leaves:
        one_hot = (at == rows - m * leaf_size).astype(f32).astype(bf16)
        x_copies[m].wait()
        picked = picked + lax.dot_general(one_hot, x[m], columns, preferred_element_type=f32)
    out[:skel, :] = picked.astype(bf16)
    total = jnp.zeros((q.shape[0], skel), f32)
    q_copy.wait()
    for m in leaves:
        l_copies[m].wait()
        leaf_up = dot(q[:, m * leaf_size : (m + 1) * leaf_size], leaf_w[m]).astype(bf16)
        m_copies[m].wait()
        total = total + dot(leaf_up, mid_w[m * skel : (m + 1) * skel, :])
    mid_up = total.astype(bf16)
    t_copy.wait()
    top = dot(mid_up, top_w[...])
    row = store_halves(out, skel, mid_up)
    store_halves(out, row, top.astype(bf16))


def up(points, charges, leaf_interp, interp_mid, interp_top, skel_leaf, skel_mid):
    leaf_dev, _, skel = leaf_interp.shape
    rhs = charges.shape[0]
    rows = skel + 2 * rhs * (skel // LANES)
    sem = pltpu.SemaphoreType.DMA
    whole = (points, charges, leaf_interp, interp_mid, interp_top)
    return call(
        up_kernel,
        jax.ShapeDtypeStruct((rows, LANES), bf16),
        [in_hbm()] * 5 + [vmem()] * 2,
        cost(3e9, 5e6),
        whole + (skel_leaf, skel_mid),
        scratch=[pltpu.VMEM(a.shape, bf16) for a in whole]
        + [sem((leaf_dev,)), sem((leaf_dev,)), sem((leaf_dev,)), sem, sem],
        own=None,
    )


def far_kernel(partners, mids, tops, interp_top, interp_mid, leaf_interp, out):
    leaf_dev, _, skel = leaf_interp.shape
    rhs = out.shape[1]

    def pair(source_ref, target, target_sq):
        source = source_ref[:skel, :]
        weight = load_halves(source_ref, skel, rhs, skel)
        tile = kernel_tile(source, source_term(source), target, target_sq)
        return dot(weight, tile)

    target = tops[0, :skel, :]
    target_sq = target_term(target)
    top_sum = jnp.zeros((rhs, skel), f32)
    for other in range(1, tops.shape[0]):
        top_sum = top_sum + pair(tops.at[other], target, target_sq)
    target = mids[0, :skel, :]
    target_sq = target_term(target)
    mid_sum = jnp.zeros((rhs, skel), f32)
    for at in range(partners.shape[0]):
        mid_sum = mid_sum + pair(mids.at[partners[at]], target, target_sq)
    total = (mid_sum + dot_rows(top_sum.astype(bf16), interp_top[...])).astype(bf16)
    for m in range(leaf_dev):
        leaf_down = dot_rows(total, interp_mid[m * skel : (m + 1) * skel, :]).astype(bf16)
        out[m] = dot_rows(leaf_down, leaf_interp[m])


def far(partners, mids, tops, interp_top, interp_mid, leaf_interp):
    leaf_dev, leaf_size, skel = leaf_interp.shape
    rhs = (mids.shape[1] - skel) // (2 * (skel // LANES))
    return call(
        far_kernel,
        jax.ShapeDtypeStruct((leaf_dev, rhs, leaf_size), f32),
        [smem()] + [vmem()] * 5,
        cost(1e9, 6e6, 5e5),
        (partners, mids, tops, interp_top, interp_mid, leaf_interp),
        own=1 << 20,
    )


def swapped(value, axis, size, distance):
    return lax.ppermute(value, axis, [(i, i ^ distance) for i in range(size)])


def share_halves(value, axis, size):
    half = size // 2
    pair = jnp.stack((value, swapped(value, axis, size, half)))
    others = [swapped(pair, axis, size, d) for d in range(1, half)]
    return jnp.concatenate([pair] + others, axis=0)


def place(distance, size):
    half = size // 2
    return distance % half * 2 + distance // half


def share(value, axis, size):
    gathered = value[None]
    while gathered.shape[0] < size:
        at = gathered.shape[0]
        other = swapped(gathered, axis, size, at)
        gathered = jnp.concatenate((gathered, other), axis=0)
    return gathered


def across(group):
    half = group // 2
    cuts = [half, half + max(half // 4, 1), half + half // 2, half + half * 3 // 4, group]
    return [list(range(*cut)) for cut in zip(cuts, cuts[1:])]


def near_spans(group):
    half = group // 2
    spans = [(half, half + half // 2), (1, half)]
    spans += [(half + half // 2, half + half * 3 // 4), (half + half * 3 // 4, group)]
    return [span for span in spans if span[1] > span[0]]


def body(
    points,
    charges,
    near_leaves,
    leaf_interpolant,
    skel_leaf,
    interp_mid,
    skel_mid,
    mid_partners,
    interp_top,
    skel_top,
):
    group = lax.axis_size("sub")
    groups = lax.axis_size("leaf")
    self_index = lax.axis_index("sub")
    leaf_dev, leaf_size, skel = leaf_interpolant.shape
    coords = points.shape[1]
    rhs = charges.shape[1]
    near_count = near_leaves.shape[1]
    group_first = lax.axis_index("leaf") * group
    blocks = points.reshape(leaf_dev, leaf_size, coords)
    charges_t = charges.T

    where = jnp.stack((group_first * leaf_dev, self_index)).astype(i32)
    chosen, pool = want(near_leaves, where, leaf_dev, group)
    handed = lax.all_to_all(chosen, "sub", split_axis=0, concat_axis=0, tiled=True)

    message = up(
        blocks, charges_t, leaf_interpolant, interp_mid[0], interp_top[0], skel_leaf, skel_mid
    )

    early = across(group)[0]
    got = {}
    for distances in (early, [d for d in range(1, group) if d not in early]):
        asked = pack(where, handed, blocks, charges_t, distances)
        for distance, one in zip(distances, asked):
            got[distance] = swapped(one, "sub", group, distance)

    half = leaf_dev // 2
    first, tsq = near_local(pool, near_count, blocks, charges_t, (0, half))
    second = near_local(pool, near_count, blocks, charges_t, (half, leaf_dev), tsq)
    sums = [first, second]

    mids = share_halves(message, "sub", group)
    per = rhs * (skel // LANES)
    picked = skel_top[0]
    node = place(jnp.bitwise_xor(picked // skel, self_index), group)
    top_points = mids.reshape(-1, LANES)[node * mids.shape[1] + picked % skel]
    top_weight = jnp.sum(mids[:, skel + per :, :].astype(f32), axis=0).astype(bf16)
    tops = share(jnp.concatenate((top_points, top_weight), axis=0), "leaf", groups)

    partners = place(jnp.bitwise_xor(mid_partners[0] - group_first, self_index), group)
    distant = far(partners, mids, tops, interp_top[0], interp_mid[0], leaf_interpolant)
    spans = near_spans(group)
    for at, span in enumerate(spans):
        stage = "first" if at == 0 else "middle"
        if at == len(spans) - 1:
            stage = "last"
            sums.append(distant)
        part = [got[distance] for distance in range(*span)]
        sums = [near_remote(pool, near_count, blocks, tsq, span[0], part, sums, stage)]
    return sums[0].T


def solution(mesh):
    placed = (
        P(("leaf", "sub"), None),
        P(("leaf", "sub"), None),
        P(("leaf", "sub"), None),
        P(("leaf", "sub"), None, None),
        P(("leaf", "sub"), None),
        P(("leaf", "sub"), None, None),
        P(("leaf", "sub"), None),
        P(("leaf", "sub"), None),
        P("leaf", "sub", None),
        P("leaf", None),
    )
    return jax.shard_map(
        body, mesh=mesh, in_specs=placed, out_specs=P(("leaf", "sub"), None), check_vma=False
    )
```

```python
import functools
import math

import jax
import jax.numpy as jnp
from jax import lax
from jax.experimental import pallas as pl
from jax.experimental.pallas import tpu as pltpu
from jax.sharding import PartitionSpec as P


CAP = 2
UNROLL = 4
LANES = 128
kernel_rate = 0.25
VMEM_BYTES = 67043328
LOG2E = math.log2(math.e)
bf16 = jnp.bfloat16
f32 = jnp.float32
i32 = jnp.int32

ROWS_ROWS = (((1,), (1,)), ((), ()))


def dot(a, b):
    return jnp.dot(a, b, preferred_element_type=f32)


def dot_rows(a, b):
    return lax.dot_general(a, b, ROWS_ROWS, preferred_element_type=f32)


def squares(x):
    xf = x.astype(f32)
    sq = xf * xf
    high = sq.astype(bf16)
    low = (sq - high.astype(f32)).astype(bf16)
    return jnp.concatenate((high, low), axis=1)


def source_term(x):
    ones = jnp.ones((2 * x.shape[1], LANES), bf16)
    return dot(squares(x), ones) * (-kernel_rate * LOG2E)


def target_term(x):
    ones = jnp.ones((8, 2 * x.shape[1]), bf16)
    return dot_rows(ones, squares(x)) * (-kernel_rate * LOG2E)


def kernel_tile(source, source_sq, target, target_sq):
    products = dot_rows(source, target)
    columns = []
    for at in range(0, target.shape[0], LANES):
        exponent = products[:, at : at + LANES] * (2.0 * kernel_rate * LOG2E) + (
            source_sq + target_sq[0:1, at : at + LANES]
        )
        columns.append(jnp.exp2(exponent).astype(bf16))
    return jnp.concatenate(columns, axis=1)


def cost(flops, bytes_accessed, transcendentals=0):
    return pl.CostEstimate(
        flops=int(flops), bytes_accessed=int(bytes_accessed), transcendentals=int(transcendentals)
    )


def room(shapes):
    total = 0
    for shape in shapes:
        count = shape.dtype.itemsize * math.prod(shape.shape[:-1])
        total += count * -(-shape.shape[-1] // LANES) * LANES
    return total


def in_hbm():
    return pl.BlockSpec(memory_space=pltpu.HBM)


def copy_in(source, target, sem):
    made = pltpu.make_async_copy(source, target, sem)
    made.start()
    return made


def call(kernel, out_shape, in_specs, estimate, operands, scratch=(), own=0, outs=None, alias=None):
    several = isinstance(out_shape, (tuple, list))
    shapes = out_shape if several else [out_shape]
    specs = outs or [vmem()] * len(shapes)
    grant = room(operands) + room(shapes) + own + (2 << 20) if own is not None else VMEM_BYTES
    return pl.pallas_call(
        kernel,
        out_shape=out_shape,
        in_specs=in_specs,
        out_specs=specs if several else specs[0],
        scratch_shapes=list(scratch),
        input_output_aliases=alias or {},
        compiler_params=pltpu.CompilerParams(vmem_limit_bytes=grant),
        cost_estimate=estimate,
    )(*operands)


def vmem():
    return pl.BlockSpec(memory_space=pltpu.VMEM)


def smem():
    return pl.BlockSpec(memory_space=pltpu.SMEM)


def want_kernel(leaf_dev, group, where, near, chosen, pool):
    base, self_index = where[0], where[1]
    rows, near_count = near.shape
    width = max(LANES, group * leaf_dev)
    local = near[...] - base
    lane = lax.broadcasted_iota(i32, (rows, width), 1)
    member = lax.rem(lane, leaf_dev)
    owner = lax.div(lane, leaf_dev)
    named = jnp.zeros((rows, width), f32)
    for entry in range(near_count):
        named = jnp.maximum(named, (local[:, entry : entry + 1] == lane).astype(f32))
    wanted = jnp.max(named, axis=0, keepdims=True)
    wanted = jnp.where(owner == self_index, 0.0, jnp.broadcast_to(wanted, (rows, width)))
    row_id = lax.broadcasted_iota(i32, (width, width), 0)
    col_id = lax.broadcasted_iota(i32, (width, width), 1)
    before = (lax.div(row_id, leaf_dev) == lax.div(col_id, leaf_dev)) & (row_id < col_id)
    rank = dot(wanted.astype(bf16), before.astype(f32).astype(bf16))
    slot = lax.broadcasted_iota(i32, (rows, width), 0).astype(f32)
    picked = jnp.where((wanted > 0.0) & (rank == slot), member.astype(f32), 0.0)
    owner_row = lax.broadcasted_iota(i32, (group, width), 0)
    owner_of = lax.div(lax.broadcasted_iota(i32, (group, width), 1), leaf_dev)
    belongs = (owner_row == owner_of).astype(f32).astype(bf16)
    chosen[...] = dot_rows(belongs, picked.astype(bf16)).astype(i32)
    place = jnp.zeros((rows, LANES), i32)
    short_lane = lax.broadcasted_iota(i32, (rows, LANES), 1)
    for entry in range(near_count):
        ids = local[:, entry : entry + 1]
        at = jnp.sum(jnp.where(ids == lane, rank, 0.0), axis=1, keepdims=True).astype(i32)
        distance = jnp.bitwise_xor(lax.div(ids, leaf_dev), self_index)
        index = jnp.where(
            distance == 0,
            lax.rem(ids, leaf_dev),
            leaf_dev + distance * CAP + jnp.clip(at, 0, CAP - 1),
        )
        place = jnp.where(short_lane == entry, index, place)
    pool[...] = place


def want(near_leaves, where, leaf_dev, group):
    rows = near_leaves.shape[0]
    return call(
        functools.partial(want_kernel, leaf_dev, group),
        [jax.ShapeDtypeStruct((group, rows), i32), jax.ShapeDtypeStruct((rows, LANES), i32)],
        [smem(), vmem()],
        cost(1e6, 1e5),
        (where, near_leaves),
        own=None,
    )


def pack_kernel(leaf_size, distances, count, where, handed, points, charges, *refs):
    blocks, refs = refs[:count], refs[count:]
    outs, (x, q, mid, sem_x, sem_q, sem_m, sem_out) = refs[: len(distances)], refs[len(distances) :]
    self_index = where[1]
    rhs = charges.shape[0]
    rows = leaf_size + leaf_size // LANES * rhs
    taken, given = [], []
    mid_copies = [copy_in(block, mid.at[at], sem_m.at[at]) for at, block in enumerate(blocks)]
    for at, distance in enumerate(distances):
        peer = jnp.bitwise_xor(self_index, distance)
        for slot in range(CAP):
            leaf = handed[peer, slot]
            lanes = pl.ds(pl.multiple_of(leaf * leaf_size, leaf_size), leaf_size)
            put = at * CAP + slot
            taken.append(
                (
                    copy_in(points.at[leaf], x.at[put], sem_x.at[put]),
                    copy_in(charges.at[:, lanes], q.at[put], sem_q.at[put]),
                )
            )
    for waited in mid_copies:
        waited.wait()
    tiles = leaf_size // LANES
    for at, out in enumerate(outs):
        for slot in range(CAP):
            put = at * CAP + slot
            base = slot * rows
            taken[put][0].wait()
            given.append(
                copy_in(x.at[put], out.at[base : base + leaf_size, :], sem_out.at[put, 0])
            )
            taken[put][1].wait()
            for tile in range(tiles):
                row = base + leaf_size + tile * rhs
                lanes = pl.ds(tile * LANES, LANES)
                given.append(
                    copy_in(
                        q.at[put, :, lanes], out.at[row : row + rhs, :], sem_out.at[put, 1 + tile]
                    )
                )
        for block in range(count):
            row = CAP * rows + block * mid.shape[1]
            given.append(
                copy_in(
                    mid.at[block],
                    out.at[row : row + mid.shape[1], :],
                    sem_out.at[at * CAP, 1 + tiles + block],
                )
            )
    for one in given:
        one.wait()


def pack(where, handed, points, charges, distances, *blocks):
    _, leaf_size, coords = points.shape
    rhs = charges.shape[0]
    rows = CAP * (leaf_size + leaf_size // LANES * rhs)
    each = blocks[0].shape[0] if blocks else 16
    rows += len(blocks) * each
    places = len(distances) * CAP
    sem = pltpu.SemaphoreType.DMA
    return call(
        functools.partial(pack_kernel, leaf_size, distances, len(blocks)),
        [jax.ShapeDtypeStruct((rows, coords), bf16) for _ in distances],
        [smem(), smem()] + [in_hbm()] * (2 + len(blocks)),
        cost(1e5, 2 * len(distances) * rows * coords * 2),
        (where, handed, points, charges) + blocks,
        scratch=[
            pltpu.VMEM((places, leaf_size, coords), bf16),
            pltpu.VMEM((places, rhs, leaf_size), bf16),
            pltpu.VMEM((max(len(blocks), 1), each, coords), bf16),
            sem((places,)),
            sem((places,)),
            sem((max(len(blocks), 1),)),
            sem((places, 1 + leaf_size // LANES + len(blocks))),
        ],
        own=None,
        outs=[in_hbm()] * len(distances),
    )


def run_pairs(pool, near_count, leaves, keep, tl, sl, tile_of, charge_of, acc, base):
    def scan(leaf, count):
        for entry in range(near_count):
            kept, source = keep(pool[leaf, entry])
            tl[count] = leaf
            sl[count] = source
            count = count + kept.astype(i32)
        return count

    count = lax.fori_loop(leaves[0], leaves[1], scan, jnp.int32(0))

    def one(at):
        target, source = tl[at], sl[at]
        acc[target - base] += dot(charge_of(source), tile_of(target, source))

    def several(step, carry):
        for k in range(UNROLL):
            one(step * UNROLL + k)
        return carry

    def single(at, carry):
        one(at)
        return carry

    whole = lax.div(count, UNROLL)
    lax.fori_loop(0, whole, several, 0)
    lax.fori_loop(whole * UNROLL, count, single, 0)


def near_cost(pairs, leaf_size, coords, rhs):
    return cost(
        pairs * 2 * leaf_size * leaf_size * 4 * (coords + rhs), 3e6, pairs * leaf_size * leaf_size
    )


def near_local_kernel(near_count, leaves, pool, points, charges, *refs):
    if leaves[0] == 0:
        out, tsq, tl, sl, x, q, ssq, acc, sem_x, sem_q, sem_out = refs
    else:
        tsq, out, tl, sl, x, q, ssq, acc, sem_x, sem_q, sem_out = refs
    leaf_dev, leaf_size, _ = points.shape
    q_copy = copy_in(charges, q, sem_q)
    x_copies = [copy_in(points.at[m], x.at[m], sem_x.at[m]) for m in range(leaf_dev)]
    acc[...] = jnp.zeros_like(acc)
    for leaf, waited in enumerate(x_copies):
        waited.wait()
        ssq[leaf] = source_term(x[leaf])
        if leaves[0] == 0:
            tsq[leaf] = target_term(x[leaf])
    q_copy.wait()

    def charge_of(source):
        at = pl.multiple_of(source * leaf_size, leaf_size)
        return q[:, pl.ds(at, leaf_size)]

    def tile_of(target, source):
        return kernel_tile(x[source], ssq[source], x[target], tsq[target])

    def keep(index):
        return index < leaf_dev, index

    run_pairs(pool, near_count, leaves, keep, tl, sl, tile_of, charge_of, acc, leaves[0])
    copy_in(acc, out, sem_out).wait()


def near_local(pool, near_count, points, charges, leaves, *tsq):
    leaf_dev, leaf_size, coords = points.shape
    rhs = charges.shape[0]
    span = leaves[1] - leaves[0]
    result = jax.ShapeDtypeStruct((span, rhs, leaf_size), f32)
    terms = jax.ShapeDtypeStruct((leaf_dev, 8, leaf_size), f32)
    return call(
        functools.partial(near_local_kernel, near_count, leaves),
        result if tsq else [result, terms],
        [smem(), in_hbm(), in_hbm()] + [vmem()] * len(tsq),
        near_cost(span * near_count / 2, leaf_size, coords, rhs),
        (pool, points, charges) + tsq,
        scratch=[
            pltpu.SMEM((leaf_dev * near_count + 1,), i32),
            pltpu.SMEM((leaf_dev * near_count + 1,), i32),
            pltpu.VMEM(points.shape, bf16),
            pltpu.VMEM(charges.shape, bf16),
            pltpu.VMEM((leaf_dev, leaf_size, LANES), f32),
            pltpu.VMEM((span, rhs, leaf_size), f32),
            pltpu.SemaphoreType.DMA((leaf_dev,)),
            pltpu.SemaphoreType.DMA,
            pltpu.SemaphoreType.DMA,
        ],
        own=None,
        outs=[in_hbm()] if tsq else [in_hbm(), vmem()],
    )


def near_remote_kernel(near_count, first, parts, stage, pool, points, tsq, *refs):
    got, refs = refs[:parts], refs[parts:]
    taken = 2 if stage == "first" else 1
    inits, refs = refs[:taken], refs[taken:]
    acc, tl, sl, x, pts, ssq, qs, sem_got, sem_x, sem_acc = refs
    leaf_dev, leaf_size, _ = points.shape
    rhs = acc.shape[1]
    tiles = leaf_size // LANES

    moves = []
    for part, message in enumerate(got):
        for slot in range(CAP):
            at = part * CAP + slot
            base = slot * (leaf_size + tiles * rhs)
            one = [copy_in(message.at[base : base + leaf_size, :], pts.at[at], sem_got.at[at, 0])]
            for tile in range(tiles):
                row = base + leaf_size + tile * rhs
                lanes = pl.ds(tile * LANES, LANES)
                one.append(
                    copy_in(
                        message.at[row : row + rhs, :], qs.at[at, :, lanes], sem_got.at[at, 1 + tile]
                    )
                )
            moves.append(one)
    x_copy = copy_in(points, x, sem_x)
    acc_copies = []
    if stage == "first":
        base = 0
        for at, init in enumerate(inits):
            rows = pl.ds(base, init.shape[0])
            acc_copies.append(copy_in(init, acc.at[rows], sem_acc.at[at]))
            base += init.shape[0]
    for at, one in enumerate(moves):
        one[0].wait()
        ssq[at] = source_term(pts[at])
        for move in one[1:]:
            move.wait()
    x_copy.wait()
    for move in acc_copies:
        move.wait()

    low = leaf_dev + first * CAP

    def keep(index):
        return (index >= low) & (index < low + parts * CAP), index - low

    def tile_of(target, source):
        return kernel_tile(pts[source], ssq[source], x[target], tsq[target])

    run_pairs(pool, near_count, (0, leaf_dev), keep, tl, sl, tile_of, lambda s: qs[s], acc, 0)


def near_remote(pool, near_count, points, tsq, first, got, inits, stage):
    leaf_dev, leaf_size, coords = points.shape
    rhs = inits[0].shape[1]
    places = len(got) * CAP
    sums = (leaf_dev, rhs, leaf_size)
    scratch = [
        pltpu.SMEM((leaf_dev * near_count + 1,), i32),
        pltpu.SMEM((leaf_dev * near_count + 1,), i32),
        pltpu.VMEM(points.shape, bf16),
        pltpu.VMEM((places, leaf_size, coords), bf16),
        pltpu.VMEM((places, leaf_size, LANES), f32),
        pltpu.VMEM((places, rhs, leaf_size), bf16),
        pltpu.SemaphoreType.DMA((places, 1 + leaf_size // LANES)),
        pltpu.SemaphoreType.DMA,
        pltpu.SemaphoreType.DMA((2,)),
    ]
    spec = in_hbm() if stage == "first" else vmem()
    return call(
        functools.partial(near_remote_kernel, near_count, first, len(got), stage),
        jax.ShapeDtypeStruct(sums, f32),
        [smem(), in_hbm(), vmem()] + [in_hbm()] * len(got) + [spec] * len(inits),
        near_cost(len(got) * leaf_dev, leaf_size, coords, rhs),
        (pool, points, tsq, *got, *inits),
        scratch=scratch,
        own=(leaf_dev * rhs * 4 + places * (coords * 2 + LANES * 4 + rhs * 2)) * leaf_size
        + (2 << 20),
        alias={3 + len(got): 0} if stage == "middle" else None,
    )


def store_halves(out, row, value):
    for tile in range(value.shape[1] // LANES):
        out[row : row + value.shape[0], :] = value[:, tile * LANES : (tile + 1) * LANES]
        row += value.shape[0]
    return row


def load_halves(ref, row, rows, width):
    tiles = [ref[row + t * rows : row + (t + 1) * rows, :] for t in range(width // LANES)]
    return jnp.concatenate(tiles, axis=1)


def skeleton_rows(skel_leaf, skel_mid, leaf_size):
    leaf_dev, skel = skel_leaf.shape
    column = lax.rem(skel_mid, skel)
    leaf = lax.div(skel_mid, skel)
    hit = lax.broadcasted_iota(i32, (skel, skel), 0) == column
    table = jnp.concatenate((lax.div(skel_leaf, 16), lax.rem(skel_leaf, 16)), axis=0)
    found = dot(table.astype(f32).astype(bf16), hit.astype(f32).astype(bf16))
    index = (found[:leaf_dev] * 16.0 + found[leaf_dev:]).astype(i32)
    row = lax.broadcasted_iota(i32, (leaf_dev, skel), 0)
    return jnp.sum(jnp.where(row == leaf, index + row * leaf_size, 0), axis=0, keepdims=True)


def up_kernel(*refs):
    points, charges, leaf_interp, interp_mid, interp_top, skel_leaf, skel_mid, out = refs[:8]
    x, q, leaf_w, mid_w, top_w, sem_x, sem_l, sem_m, sem_q, sem_t = refs[8:]
    leaf_dev, leaf_size, skel = leaf_interp.shape
    leaves = range(leaf_dev)
    x_copies = [copy_in(points.at[m], x.at[m], sem_x.at[m]) for m in leaves]
    q_copy = copy_in(charges, q, sem_q)
    l_copies, m_copies = [], []
    for m in leaves:
        rows = pl.ds(m * skel, skel)
        l_copies.append(copy_in(leaf_interp.at[m], leaf_w.at[m], sem_l.at[m]))
        m_copies.append(copy_in(interp_mid.at[rows], mid_w.at[rows], sem_m.at[m]))
    t_copy = copy_in(interp_top, top_w, sem_t)

    rows = skeleton_rows(skel_leaf[...], skel_mid[...], leaf_size)
    at = lax.broadcasted_iota(i32, (leaf_size, skel), 0)
    columns = (((0,), (0,)), ((), ()))
    picked = jnp.zeros((skel, x.shape[2]), f32)
    for m in leaves:
        one_hot = (at == rows - m * leaf_size).astype(f32).astype(bf16)
        x_copies[m].wait()
        picked = picked + lax.dot_general(one_hot, x[m], columns, preferred_element_type=f32)
    out[:skel, :] = picked.astype(bf16)
    total = jnp.zeros((q.shape[0], skel), f32)
    q_copy.wait()
    for m in leaves:
        l_copies[m].wait()
        leaf_up = dot(q[:, m * leaf_size : (m + 1) * leaf_size], leaf_w[m]).astype(bf16)
        m_copies[m].wait()
        total = total + dot(leaf_up, mid_w[m * skel : (m + 1) * skel, :])
    mid_up = total.astype(bf16)
    t_copy.wait()
    top = dot(mid_up, top_w[...])
    row = store_halves(out, skel, mid_up)
    store_halves(out, row, top.astype(bf16))


def up(points, charges, leaf_interp, interp_mid, interp_top, skel_leaf, skel_mid):
    leaf_dev, _, skel = leaf_interp.shape
    rhs = charges.shape[0]
    rows = skel + 2 * rhs * (skel // LANES)
    sem = pltpu.SemaphoreType.DMA
    whole = (points, charges, leaf_interp, interp_mid, interp_top)
    return call(
        up_kernel,
        jax.ShapeDtypeStruct((rows, LANES), bf16),
        [in_hbm()] * 5 + [vmem()] * 2,
        cost(3e9, 5e6),
        whole + (skel_leaf, skel_mid),
        scratch=[pltpu.VMEM(a.shape, bf16) for a in whole]
        + [sem((leaf_dev,)), sem((leaf_dev,)), sem((leaf_dev,)), sem, sem],
        own=None,
    )


def place(distance, size):
    half = size // 2
    return lax.rem(distance, half) * 2 + lax.div(distance, half)


def top_kernel(near_rows, where, skel_top, own, across_own, *refs):
    inner = len(refs) - 3
    got, (mids, out, sem) = refs[:inner], refs[inner:]
    size, rows, _ = mids.shape
    skel = skel_top.shape[1]
    copies = [copy_in(own, mids.at[0], sem.at[0]), copy_in(across_own, mids.at[1], sem.at[1])]
    for at, message in enumerate(got, 1):
        for side in range(2):
            row = near_rows + side * rows
            to = at * 2 + side
            copies.append(copy_in(message.at[row : row + rows, :], mids.at[to], sem.at[to]))
    picked = skel_top[...]
    distance = jnp.bitwise_xor(lax.div(picked, skel), where[1])
    index = place(distance, size) * skel + lax.rem(picked, skel)
    at = lax.broadcasted_iota(i32, (skel, skel), 0)
    columns = (((0,), (0,)), ((), ()))
    points = jnp.zeros((skel, mids.shape[2]), f32)
    first = skel + (rows - skel) // 2
    weight = jnp.zeros((rows - first, mids.shape[2]), f32)
    for p in range(size):
        one_hot = (at == index - p * skel).astype(f32).astype(bf16)
        copies[p].wait()
        points = points + lax.dot_general(
            one_hot, mids[p, :skel, :], columns, preferred_element_type=f32
        )
        weight = weight + mids[p, first:, :].astype(f32)
    out[:skel, :] = points.astype(bf16)
    out[skel:, :] = weight.astype(bf16)


def top_prepare(near_rows, where, skel_top, own, across_own, got):
    rows, coords = own.shape
    skel = skel_top.shape[1]
    size = 2 + 2 * len(got)
    return call(
        functools.partial(top_kernel, near_rows),
        [
            jax.ShapeDtypeStruct((size, rows, coords), bf16),
            jax.ShapeDtypeStruct((skel + (rows - skel) // 2, coords), bf16),
        ],
        [smem(), vmem()] + [in_hbm()] * (2 + len(got)),
        cost(1e9, 2e6),
        (where, skel_top, own, across_own, *got),
        scratch=[pltpu.SemaphoreType.DMA((size,))],
        own=2 << 20,
    )


def far_kernel(where, partners, mids, acc, interp_top, interp_mid, leaf_interp, *refs):
    tops, out = refs[:-1], refs[-1]
    leaf_dev, leaf_size, skel = leaf_interp.shape
    rhs = acc.shape[1]

    def pair(source_ref, target, target_sq):
        source = source_ref[:skel, :]
        weight = load_halves(source_ref, skel, rhs, skel)
        tile = kernel_tile(source, source_term(source), target, target_sq)
        return dot(weight, tile)

    target = tops[0][:skel, :]
    target_sq = target_term(target)
    top_sum = jnp.zeros((rhs, skel), f32)
    for other in tops[1:]:
        top_sum = top_sum + pair(other, target, target_sq)
    target = mids[0, :skel, :]
    target_sq = target_term(target)
    mid_sum = jnp.zeros((rhs, skel), f32)
    for at in range(partners.shape[1]):
        distance = jnp.bitwise_xor(partners[0, at] - where[2], where[1])
        mid_sum = mid_sum + pair(mids.at[place(distance, mids.shape[0])], target, target_sq)
    total = (mid_sum + dot_rows(top_sum.astype(bf16), interp_top[...])).astype(bf16)
    for m in range(leaf_dev):
        leaf_down = dot_rows(total, interp_mid[m * skel : (m + 1) * skel, :]).astype(bf16)
        distant = dot_rows(leaf_down, leaf_interp[m])
        out[:, m * leaf_size : (m + 1) * leaf_size] = acc[m] + distant


def far(where, partners, mids, acc, tops, interp_top, interp_mid, leaf_interp):
    leaf_dev, leaf_size, _ = leaf_interp.shape
    rhs = acc.shape[1]
    return call(
        far_kernel,
        jax.ShapeDtypeStruct((rhs, leaf_dev * leaf_size), f32),
        [smem()] * 2 + [vmem()] * (5 + len(tops)),
        cost(1e9, 6e6, 5e5),
        (where, partners, mids, acc, interp_top, interp_mid, leaf_interp, *tops),
        own=1 << 20,
    )


def swapped(value, axis, size, distance):
    return lax.ppermute(value, axis, [(i, i ^ distance) for i in range(size)])


def across(group):
    half = group // 2
    cuts = [half, half + max(half // 4, 1), half + half // 2, half + half * 3 // 4, group]
    return [list(range(*cut)) for cut in zip(cuts, cuts[1:])]


def body(
    points,
    charges,
    near_leaves,
    leaf_interpolant,
    skel_leaf,
    interp_mid,
    skel_mid,
    mid_partners,
    interp_top,
    skel_top,
):
    group = lax.axis_size("sub")
    groups = lax.axis_size("leaf")
    self_index = lax.axis_index("sub")
    leaf_dev, leaf_size, _ = leaf_interpolant.shape
    coords = points.shape[1]
    rhs = charges.shape[1]
    near_count = near_leaves.shape[1]
    group_first = lax.axis_index("leaf") * group
    blocks = points.reshape(leaf_dev, leaf_size, coords)
    charges_t = charges.T

    where = jnp.stack((group_first * leaf_dev, self_index, group_first)).astype(i32)
    chosen, pool = want(near_leaves, where, leaf_dev, group)
    handed = lax.all_to_all(chosen, "sub", split_axis=0, concat_axis=0, tiled=True)

    message = up(
        blocks, charges_t, leaf_interpolant, interp_mid[0], interp_top[0], skel_leaf, skel_mid
    )
    across_message = swapped(message, "sub", group, group // 2)

    first, second, third, last = across(group)
    inner = list(range(1, group // 2))
    got = {}
    for distances, carried in ((first, ()), (second + third + last, ()), (inner, (message, across_message))):
        asked = pack(where, handed, blocks, charges_t, distances, *carried)
        for distance, one in zip(distances, asked):
            got[distance] = swapped(one, "sub", group, distance)

    half = leaf_dev // 2
    sum0, tsq = near_local(pool, near_count, blocks, charges_t, (0, half))
    sum1 = near_local(pool, near_count, blocks, charges_t, (half, leaf_dev), tsq)
    sums = [sum0, sum1]

    near_rows = CAP * (leaf_size + leaf_size // LANES * rhs)
    mids, top_own = top_prepare(
        near_rows, where, skel_top, message, across_message, [got[d] for d in inner]
    )
    tops = [top_own]
    for distance in range(1, groups):
        tops.append(swapped(top_own, "leaf", groups, distance))

    for at, span in enumerate((first + second, inner, third + last)):
        stage = "first" if at == 0 else "middle"
        part = [got[distance] for distance in span]
        sums = [near_remote(pool, near_count, blocks, tsq, span[0], part, sums, stage)]
    total = far(
        where, mid_partners, mids, sums[0], tops, interp_top[0], interp_mid[0], leaf_interpolant
    )
    return total.T


def solution(mesh):
    placed = (
        P(("leaf", "sub"), None),
        P(("leaf", "sub"), None),
        P(("leaf", "sub"), None),
        P(("leaf", "sub"), None, None),
        P(("leaf", "sub"), None),
        P(("leaf", "sub"), None, None),
        P(("leaf", "sub"), None),
        P(("leaf", "sub"), None),
        P("leaf", "sub", None),
        P("leaf", None),
    )
    return jax.shard_map(
        body, mesh=mesh, in_specs=placed, out_specs=P(("leaf", "sub"), None), check_vma=False
    )
```

```python
import functools
import math

import jax
import jax.numpy as jnp
from jax import lax
from jax.experimental import pallas as pl
from jax.experimental.pallas import tpu as pltpu
from jax.sharding import PartitionSpec as P


CAP = 2
UNROLL = 4
LANES = 128
kernel_rate = 0.25
VMEM_BYTES = 67043328
LOG2E = math.log2(math.e)
bf16 = jnp.bfloat16
f32 = jnp.float32
i32 = jnp.int32

ROWS_ROWS = (((1,), (1,)), ((), ()))


def dot(a, b):
    return jnp.dot(a, b, preferred_element_type=f32)


def dot_rows(a, b):
    return lax.dot_general(a, b, ROWS_ROWS, preferred_element_type=f32)


def squares(x):
    xf = x.astype(f32)
    sq = xf * xf
    high = sq.astype(bf16)
    low = (sq - high.astype(f32)).astype(bf16)
    return jnp.concatenate((high, low), axis=1)


def source_term(x):
    xf = x.astype(f32)
    total = jnp.sum(xf * xf, axis=1, keepdims=True) * (-kernel_rate * LOG2E)
    return jnp.broadcast_to(total, (x.shape[0], LANES))


def target_term(x):
    ones = jnp.ones((8, 2 * x.shape[1]), bf16)
    return dot_rows(ones, squares(x)) * (-kernel_rate * LOG2E)


def kernel_tile(source, source_sq, target, target_sq):
    products = dot_rows(source, target)
    columns = []
    for at in range(0, target.shape[0], LANES):
        exponent = products[:, at : at + LANES] * (2.0 * kernel_rate * LOG2E) + (
            source_sq + target_sq[0:1, at : at + LANES]
        )
        columns.append(jnp.exp2(exponent).astype(bf16))
    return jnp.concatenate(columns, axis=1)


def cost(flops, bytes_accessed, transcendentals=0):
    return pl.CostEstimate(
        flops=int(flops), bytes_accessed=int(bytes_accessed), transcendentals=int(transcendentals)
    )


def room(shapes):
    total = 0
    for shape in shapes:
        count = shape.dtype.itemsize * math.prod(shape.shape[:-1])
        total += count * -(-shape.shape[-1] // LANES) * LANES
    return total


def in_hbm():
    return pl.BlockSpec(memory_space=pltpu.HBM)


def copy_in(source, target, sem):
    made = pltpu.make_async_copy(source, target, sem)
    made.start()
    return made


def call(kernel, out_shape, in_specs, estimate, operands, scratch=(), own=0, outs=None, alias=None):
    several = isinstance(out_shape, (tuple, list))
    shapes = out_shape if several else [out_shape]
    specs = outs or [vmem()] * len(shapes)
    grant = room(operands) + room(shapes) + own + (2 << 20) if own is not None else VMEM_BYTES
    return pl.pallas_call(
        kernel,
        out_shape=out_shape,
        in_specs=in_specs,
        out_specs=specs if several else specs[0],
        scratch_shapes=list(scratch),
        input_output_aliases=alias or {},
        compiler_params=pltpu.CompilerParams(vmem_limit_bytes=grant),
        cost_estimate=estimate,
    )(*operands)


def vmem():
    return pl.BlockSpec(memory_space=pltpu.VMEM)


def smem():
    return pl.BlockSpec(memory_space=pltpu.SMEM)


def want_kernel(leaf_dev, group, where, near, chosen, pool):
    base, self_index = where[0], where[1]
    rows, near_count = near.shape
    width = max(LANES, group * leaf_dev)
    local = near[...] - base
    lane = lax.broadcasted_iota(i32, (rows, width), 1)
    member = lax.rem(lane, leaf_dev)
    owner = lax.div(lane, leaf_dev)
    named = jnp.zeros((rows, width), f32)
    for entry in range(near_count):
        named = jnp.maximum(named, (local[:, entry : entry + 1] == lane).astype(f32))
    wanted = jnp.max(named, axis=0, keepdims=True)
    wanted = jnp.where(owner == self_index, 0.0, jnp.broadcast_to(wanted, (rows, width)))
    row_id = lax.broadcasted_iota(i32, (width, width), 0)
    col_id = lax.broadcasted_iota(i32, (width, width), 1)
    before = (lax.div(row_id, leaf_dev) == lax.div(col_id, leaf_dev)) & (row_id < col_id)
    rank = dot(wanted.astype(bf16), before.astype(f32).astype(bf16))
    slot = lax.broadcasted_iota(i32, (rows, width), 0).astype(f32)
    picked = jnp.where((wanted > 0.0) & (rank == slot), member.astype(f32), 0.0)
    owner_row = lax.broadcasted_iota(i32, (group, width), 0)
    owner_of = lax.div(lax.broadcasted_iota(i32, (group, width), 1), leaf_dev)
    belongs = (owner_row == owner_of).astype(f32).astype(bf16)
    chosen[...] = dot_rows(belongs, picked.astype(bf16)).astype(i32)
    place = jnp.zeros((rows, LANES), i32)
    short_lane = lax.broadcasted_iota(i32, (rows, LANES), 1)
    for entry in range(near_count):
        ids = local[:, entry : entry + 1]
        at = jnp.sum(jnp.where(ids == lane, rank, 0.0), axis=1, keepdims=True).astype(i32)
        distance = jnp.bitwise_xor(lax.div(ids, leaf_dev), self_index)
        index = jnp.where(
            distance == 0,
            lax.rem(ids, leaf_dev),
            leaf_dev + distance * CAP + jnp.clip(at, 0, CAP - 1),
        )
        place = jnp.where(short_lane == entry, index, place)
    pool[...] = place


def want(near_leaves, where, leaf_dev, group):
    rows = near_leaves.shape[0]
    return call(
        functools.partial(want_kernel, leaf_dev, group),
        [jax.ShapeDtypeStruct((group, rows), i32), jax.ShapeDtypeStruct((rows, LANES), i32)],
        [smem(), vmem()],
        cost(1e6, 1e5),
        (where, near_leaves),
        own=None,
    )


def pack_kernel(leaf_size, distances, count, where, handed, points, charges, *refs):
    blocks, refs = refs[:count], refs[count:]
    outs, refs = refs[: len(distances)], refs[len(distances) :]
    if count:
        pair, refs = refs[0], refs[1:]
    x, q, mid, sem_x, sem_q, sem_m, sem_out = refs
    self_index = where[1]
    rhs = charges.shape[0]
    rows = leaf_size + leaf_size // LANES * rhs
    taken, given = [], []
    mid_copies = [copy_in(block, mid.at[at], sem_m.at[at]) for at, block in enumerate(blocks)]
    for at, distance in enumerate(distances):
        peer = jnp.bitwise_xor(self_index, distance)
        for slot in range(CAP):
            leaf = handed[peer, slot]
            lanes = pl.ds(pl.multiple_of(leaf * leaf_size, leaf_size), leaf_size)
            put = at * CAP + slot
            taken.append(
                (
                    copy_in(points.at[leaf], x.at[put], sem_x.at[put]),
                    copy_in(charges.at[:, lanes], q.at[put], sem_q.at[put]),
                )
            )
    for at, waited in enumerate(mid_copies):
        waited.wait()
        to = pair.at[at * mid.shape[1] : (at + 1) * mid.shape[1], :]
        given.append(copy_in(mid.at[at], to, sem_m.at[at]))
    tiles = leaf_size // LANES
    for at, out in enumerate(outs):
        for slot in range(CAP):
            put = at * CAP + slot
            base = slot * rows
            taken[put][0].wait()
            given.append(
                copy_in(x.at[put], out.at[base : base + leaf_size, :], sem_out.at[put, 0])
            )
            taken[put][1].wait()
            for tile in range(tiles):
                row = base + leaf_size + tile * rhs
                lanes = pl.ds(tile * LANES, LANES)
                given.append(
                    copy_in(
                        q.at[put, :, lanes], out.at[row : row + rhs, :], sem_out.at[put, 1 + tile]
                    )
                )
    for one in given:
        one.wait()


def pack(where, handed, points, charges, distances, *blocks):
    _, leaf_size, coords = points.shape
    rhs = charges.shape[0]
    rows = CAP * (leaf_size + leaf_size // LANES * rhs)
    each = blocks[0].shape[0] if blocks else 16
    shapes = [(rows, coords) for _ in distances]
    if blocks:
        shapes.append((len(blocks) * each, coords))
    places = len(distances) * CAP
    sem = pltpu.SemaphoreType.DMA
    return call(
        functools.partial(pack_kernel, leaf_size, distances, len(blocks)),
        [jax.ShapeDtypeStruct(shape, bf16) for shape in shapes],
        [smem(), smem()] + [in_hbm()] * (2 + len(blocks)),
        cost(1e5, 2 * len(distances) * rows * coords * 2),
        (where, handed, points, charges) + blocks,
        scratch=[
            pltpu.VMEM((places, leaf_size, coords), bf16),
            pltpu.VMEM((places, rhs, leaf_size), bf16),
            pltpu.VMEM((max(len(blocks), 1), each, coords), bf16),
            sem((places,)),
            sem((places,)),
            sem((max(len(blocks), 1),)),
            sem((places, 1 + leaf_size // LANES)),
        ],
        own=None,
        outs=[in_hbm()] * len(shapes),
    )


def run_pairs(pool, near_count, leaves, keep, tl, sl, tile_of, charge_of, acc, base):
    def scan(leaf, count):
        for entry in range(near_count):
            kept, source = keep(pool[leaf, entry])
            tl[count] = leaf
            sl[count] = source
            count = count + kept.astype(i32)
        return count

    count = lax.fori_loop(leaves[0], leaves[1], scan, jnp.int32(0))

    def one(at):
        target, source = tl[at], sl[at]
        acc[target - base] += dot(charge_of(source), tile_of(target, source))

    def several(step, carry):
        for k in range(UNROLL):
            one(step * UNROLL + k)
        return carry

    def single(at, carry):
        one(at)
        return carry

    whole = lax.div(count, UNROLL)
    lax.fori_loop(0, whole, several, 0)
    lax.fori_loop(whole * UNROLL, count, single, 0)


def near_cost(pairs, leaf_size, coords, rhs):
    return cost(
        pairs * 2 * leaf_size * leaf_size * 4 * (coords + rhs), 3e6, pairs * leaf_size * leaf_size
    )


def near_local_kernel(near_count, leaves, pool, points, charges, *refs):
    if leaves[0] == 0:
        out, tsq, tl, sl, x, q, ssq, acc, sem_x, sem_q, sem_out = refs
    else:
        tsq, out, tl, sl, x, q, ssq, acc, sem_x, sem_q, sem_out = refs
    leaf_dev, leaf_size, _ = points.shape
    q_copy = copy_in(charges, q, sem_q)
    x_copies = [copy_in(points.at[m], x.at[m], sem_x.at[m]) for m in range(leaf_dev)]
    acc[...] = jnp.zeros_like(acc)
    for leaf, waited in enumerate(x_copies):
        waited.wait()
        ssq[leaf] = source_term(x[leaf])
        if leaves[0] == 0:
            tsq[leaf] = target_term(x[leaf])
    q_copy.wait()

    def charge_of(source):
        at = pl.multiple_of(source * leaf_size, leaf_size)
        return q[:, pl.ds(at, leaf_size)]

    def tile_of(target, source):
        return kernel_tile(x[source], ssq[source], x[target], tsq[target])

    def keep(index):
        return index < leaf_dev, index

    run_pairs(pool, near_count, leaves, keep, tl, sl, tile_of, charge_of, acc, leaves[0])
    copy_in(acc, out, sem_out).wait()


def near_local(pool, near_count, points, charges, leaves, *tsq):
    leaf_dev, leaf_size, coords = points.shape
    rhs = charges.shape[0]
    span = leaves[1] - leaves[0]
    result = jax.ShapeDtypeStruct((span, rhs, leaf_size), f32)
    terms = jax.ShapeDtypeStruct((leaf_dev, 8, leaf_size), f32)
    return call(
        functools.partial(near_local_kernel, near_count, leaves),
        result if tsq else [result, terms],
        [smem(), in_hbm(), in_hbm()] + [vmem()] * len(tsq),
        near_cost(span * near_count / 2, leaf_size, coords, rhs),
        (pool, points, charges) + tsq,
        scratch=[
            pltpu.SMEM((leaf_dev * near_count + 1,), i32),
            pltpu.SMEM((leaf_dev * near_count + 1,), i32),
            pltpu.VMEM(points.shape, bf16),
            pltpu.VMEM(charges.shape, bf16),
            pltpu.VMEM((leaf_dev, leaf_size, LANES), f32),
            pltpu.VMEM((span, rhs, leaf_size), f32),
            pltpu.SemaphoreType.DMA((leaf_dev,)),
            pltpu.SemaphoreType.DMA,
            pltpu.SemaphoreType.DMA,
        ],
        own=None,
        outs=[in_hbm()] if tsq else [in_hbm(), vmem()],
    )


def near_remote_kernel(near_count, first, parts, stage, pool, points, tsq, *refs):
    got, refs = refs[:parts], refs[parts:]
    taken = 2 if stage == "first" else 1
    inits, refs = refs[:taken], refs[taken:]
    acc, tl, sl, x, pts, ssq, qs, sem_got, sem_x, sem_acc = refs
    leaf_dev, leaf_size, _ = points.shape
    rhs = acc.shape[1]
    tiles = leaf_size // LANES

    moves = []
    for part, message in enumerate(got):
        for slot in range(CAP):
            at = part * CAP + slot
            base = slot * (leaf_size + tiles * rhs)
            one = [copy_in(message.at[base : base + leaf_size, :], pts.at[at], sem_got.at[at, 0])]
            for tile in range(tiles):
                row = base + leaf_size + tile * rhs
                lanes = pl.ds(tile * LANES, LANES)
                one.append(
                    copy_in(
                        message.at[row : row + rhs, :], qs.at[at, :, lanes], sem_got.at[at, 1 + tile]
                    )
                )
            moves.append(one)
    x_copy = copy_in(points, x, sem_x)
    acc_copies = []
    if stage == "first":
        base = 0
        for at, init in enumerate(inits):
            rows = pl.ds(base, init.shape[0])
            acc_copies.append(copy_in(init, acc.at[rows], sem_acc.at[at]))
            base += init.shape[0]
    for at, one in enumerate(moves):
        one[0].wait()
        ssq[at] = source_term(pts[at])
        for move in one[1:]:
            move.wait()
    x_copy.wait()
    for move in acc_copies:
        move.wait()

    low = leaf_dev + first * CAP

    def keep(index):
        return (index >= low) & (index < low + parts * CAP), index - low

    def tile_of(target, source):
        return kernel_tile(pts[source], ssq[source], x[target], tsq[target])

    run_pairs(pool, near_count, (0, leaf_dev), keep, tl, sl, tile_of, lambda s: qs[s], acc, 0)


def near_remote(pool, near_count, points, tsq, first, got, inits, stage):
    leaf_dev, leaf_size, coords = points.shape
    rhs = inits[0].shape[1]
    places = len(got) * CAP
    sums = (leaf_dev, rhs, leaf_size)
    scratch = [
        pltpu.SMEM((leaf_dev * near_count + 1,), i32),
        pltpu.SMEM((leaf_dev * near_count + 1,), i32),
        pltpu.VMEM(points.shape, bf16),
        pltpu.VMEM((places, leaf_size, coords), bf16),
        pltpu.VMEM((places, leaf_size, LANES), f32),
        pltpu.VMEM((places, rhs, leaf_size), bf16),
        pltpu.SemaphoreType.DMA((places, 1 + leaf_size // LANES)),
        pltpu.SemaphoreType.DMA,
        pltpu.SemaphoreType.DMA((2,)),
    ]
    spec = in_hbm() if stage == "first" else vmem()
    return call(
        functools.partial(near_remote_kernel, near_count, first, len(got), stage),
        jax.ShapeDtypeStruct(sums, f32),
        [smem(), in_hbm(), vmem()] + [in_hbm()] * len(got) + [spec] * len(inits),
        near_cost(len(got) * leaf_dev, leaf_size, coords, rhs),
        (pool, points, tsq, *got, *inits),
        scratch=scratch,
        own=None
        if stage == "first"
        else (leaf_dev * rhs * 4 + places * (coords * 2 + LANES * 4 + rhs * 2)) * leaf_size
        + (2 << 20),
        alias={3 + len(got): 0} if stage == "middle" else None,
    )


def store_halves(out, row, value):
    for tile in range(value.shape[1] // LANES):
        out[row : row + value.shape[0], :] = value[:, tile * LANES : (tile + 1) * LANES]
        row += value.shape[0]
    return row


def load_halves(ref, row, rows, width):
    tiles = [ref[row + t * rows : row + (t + 1) * rows, :] for t in range(width // LANES)]
    return jnp.concatenate(tiles, axis=1)


def skeleton_rows(skel_leaf, skel_mid, leaf_size):
    leaf_dev, skel = skel_leaf.shape
    column = lax.rem(skel_mid, skel)
    leaf = lax.div(skel_mid, skel)
    hit = lax.broadcasted_iota(i32, (skel, skel), 0) == column
    table = jnp.concatenate((lax.div(skel_leaf, 16), lax.rem(skel_leaf, 16)), axis=0)
    found = dot(table.astype(f32).astype(bf16), hit.astype(f32).astype(bf16))
    index = (found[:leaf_dev] * 16.0 + found[leaf_dev:]).astype(i32)
    row = lax.broadcasted_iota(i32, (leaf_dev, skel), 0)
    return jnp.sum(jnp.where(row == leaf, index + row * leaf_size, 0), axis=0, keepdims=True)


def as_column(row):
    return jnp.broadcast_to(row.astype(f32), (LANES, row.shape[1])).T.astype(i32)


def pick_rows(index, base, block):
    lane = lax.broadcasted_iota(i32, index.shape, 1)
    tiles = [
        (index == lane + (base + at)).astype(f32).astype(bf16)
        for at in range(0, block.shape[0], LANES)
    ]
    return dot(jnp.concatenate(tiles, axis=1), block)


def up_kernel(*refs):
    points, charges, leaf_interp, interp_mid, interp_top, skel_leaf, skel_mid, out = refs[:8]
    x, q, leaf_w, mid_w, top_w, sem_x, sem_l, sem_m, sem_q, sem_t = refs[8:]
    leaf_dev, leaf_size, skel = leaf_interp.shape
    leaves = range(leaf_dev)
    x_copies = [copy_in(points.at[m], x.at[m], sem_x.at[m]) for m in leaves]
    q_copy = copy_in(charges, q, sem_q)
    l_copies, m_copies = [], []
    for m in leaves:
        rows = pl.ds(m * skel, skel)
        l_copies.append(copy_in(leaf_interp.at[m], leaf_w.at[m], sem_l.at[m]))
        m_copies.append(copy_in(interp_mid.at[rows], mid_w.at[rows], sem_m.at[m]))
    t_copy = copy_in(interp_top, top_w, sem_t)

    rows = as_column(skeleton_rows(skel_leaf[...], skel_mid[...], leaf_size))
    picked = jnp.zeros((skel, x.shape[2]), f32)
    for m in leaves:
        x_copies[m].wait()
        picked = picked + pick_rows(rows, m * leaf_size, x[m])
    out[:skel, :] = picked.astype(bf16)
    total = jnp.zeros((q.shape[0], skel), f32)
    q_copy.wait()
    for m in leaves:
        l_copies[m].wait()
        leaf_up = dot(q[:, m * leaf_size : (m + 1) * leaf_size], leaf_w[m]).astype(bf16)
        m_copies[m].wait()
        total = total + dot(leaf_up, mid_w[m * skel : (m + 1) * skel, :])
    mid_up = total.astype(bf16)
    t_copy.wait()
    top = dot(mid_up, top_w[...])
    row = store_halves(out, skel, mid_up)
    store_halves(out, row, top.astype(bf16))


def up(points, charges, leaf_interp, interp_mid, interp_top, skel_leaf, skel_mid):
    leaf_dev, _, skel = leaf_interp.shape
    rhs = charges.shape[0]
    rows = skel + 2 * rhs * (skel // LANES)
    sem = pltpu.SemaphoreType.DMA
    whole = (points, charges, leaf_interp, interp_mid, interp_top)
    return call(
        up_kernel,
        jax.ShapeDtypeStruct((rows, LANES), bf16),
        [in_hbm()] * 5 + [vmem()] * 2,
        cost(3e9, 5e6),
        whole + (skel_leaf, skel_mid),
        scratch=[pltpu.VMEM(a.shape, bf16) for a in whole]
        + [sem((leaf_dev,)), sem((leaf_dev,)), sem((leaf_dev,)), sem, sem],
        own=None,
    )


def place(distance, size):
    half = size // 2
    return lax.rem(distance, half) * 2 + lax.div(distance, half)


def top_kernel(where, skel_top, *refs):
    pairs, (mids, out, sem) = refs[:-3], refs[-3:]
    size, rows, _ = mids.shape
    skel = skel_top.shape[1]
    copies = []
    for to in range(size):
        row = to % 2 * rows
        source = pairs[to // 2].at[row : row + rows, :]
        copies.append(copy_in(source, mids.at[to], sem.at[to]))
    picked = skel_top[...]
    distance = jnp.bitwise_xor(lax.div(picked, skel), where[1])
    index = as_column(place(distance, size) * skel + lax.rem(picked, skel))
    points = jnp.zeros((skel, mids.shape[2]), f32)
    first = skel + (rows - skel) // 2
    weight = jnp.zeros((rows - first, mids.shape[2]), f32)
    for p in range(size):
        copies[p].wait()
        points = points + pick_rows(index, p * skel, mids[p, :skel, :])
        weight = weight + mids[p, first:, :].astype(f32)
    out[:skel, :] = points.astype(bf16)
    out[skel:, :] = weight.astype(bf16)


def top_prepare(where, skel_top, pairs):
    rows, coords = pairs[0].shape[0] // 2, pairs[0].shape[1]
    skel = skel_top.shape[1]
    size = 2 * len(pairs)
    return call(
        top_kernel,
        [
            jax.ShapeDtypeStruct((size, rows, coords), bf16),
            jax.ShapeDtypeStruct((skel + (rows - skel) // 2, coords), bf16),
        ],
        [smem(), vmem()] + [in_hbm()] * len(pairs),
        cost(1e9, 2e6),
        (where, skel_top, *pairs),
        scratch=[pltpu.SemaphoreType.DMA((size,))],
        own=2 << 20,
    )


def far_kernel(where, partners, mids, acc, interp_top, interp_mid, leaf_interp, *refs):
    tops, out = refs[:-1], refs[-1]
    leaf_dev, leaf_size, skel = leaf_interp.shape
    rhs = acc.shape[1]

    def pair(source_ref, target, target_sq):
        source = source_ref[:skel, :]
        weight = load_halves(source_ref, skel, rhs, skel)
        tile = kernel_tile(source, source_term(source), target, target_sq)
        return dot(weight, tile)

    target = tops[0][:skel, :]
    target_sq = target_term(target)
    top_sum = jnp.zeros((rhs, skel), f32)
    for other in tops[1:]:
        top_sum = top_sum + pair(other, target, target_sq)
    target = mids[0, :skel, :]
    target_sq = target_term(target)
    mid_sum = jnp.zeros((rhs, skel), f32)
    for at in range(partners.shape[1]):
        distance = jnp.bitwise_xor(partners[0, at] - where[2], where[1])
        mid_sum = mid_sum + pair(mids.at[place(distance, mids.shape[0])], target, target_sq)
    total = (mid_sum + dot_rows(top_sum.astype(bf16), interp_top[...])).astype(bf16)
    for m in range(leaf_dev):
        leaf_down = dot_rows(total, interp_mid[m * skel : (m + 1) * skel, :]).astype(bf16)
        distant = dot_rows(leaf_down, leaf_interp[m])
        out[:, m * leaf_size : (m + 1) * leaf_size] = acc[m] + distant


def far(where, partners, mids, acc, tops, interp_top, interp_mid, leaf_interp):
    leaf_dev, leaf_size, _ = leaf_interp.shape
    rhs = acc.shape[1]
    return call(
        far_kernel,
        jax.ShapeDtypeStruct((rhs, leaf_dev * leaf_size), f32),
        [smem()] * 2 + [vmem()] * (5 + len(tops)),
        cost(1e9, 6e6, 5e5),
        (where, partners, mids, acc, interp_top, interp_mid, leaf_interp, *tops),
        own=1 << 20,
    )


def swapped(value, axis, size, distance):
    return lax.ppermute(value, axis, [(i, i ^ distance) for i in range(size)])


def across(group):
    half = group // 2
    cuts = [half, half + max(half // 4, 1), half + half // 2, half + half * 3 // 4, group]
    return [list(range(*cut)) for cut in zip(cuts, cuts[1:])]


def body(
    points,
    charges,
    near_leaves,
    leaf_interpolant,
    skel_leaf,
    interp_mid,
    skel_mid,
    mid_partners,
    interp_top,
    skel_top,
):
    group = lax.axis_size("sub")
    groups = lax.axis_size("leaf")
    self_index = lax.axis_index("sub")
    leaf_dev, leaf_size, _ = leaf_interpolant.shape
    coords = points.shape[1]
    near_count = near_leaves.shape[1]
    group_first = lax.axis_index("leaf") * group
    blocks = points.reshape(leaf_dev, leaf_size, coords)
    charges_t = charges.T

    where = jnp.stack((group_first * leaf_dev, self_index, group_first)).astype(i32)
    chosen, pool = want(near_leaves, where, leaf_dev, group)
    handed = lax.all_to_all(chosen, "sub", split_axis=0, concat_axis=0, tiled=True)

    message = up(
        blocks, charges_t, leaf_interpolant, interp_mid[0], interp_top[0], skel_leaf, skel_mid
    )
    across_message = swapped(message, "sub", group, group // 2)

    first, second, third, last = across(group)
    inner = list(range(1, group // 2))
    got = {}
    for distances, carried in ((first, ()), (second + third + last, ()), (inner, (message, across_message))):
        asked = pack(where, handed, blocks, charges_t, distances, *carried)
        for distance, one in zip(distances, asked):
            got[distance] = swapped(one, "sub", group, distance)
    pair = asked[-1]
    pairs = [pair] + [swapped(pair, "sub", group, d) for d in inner]

    half = leaf_dev // 2
    sum0, tsq = near_local(pool, near_count, blocks, charges_t, (0, half))
    sum1 = near_local(pool, near_count, blocks, charges_t, (half, leaf_dev), tsq)
    sums = [sum0, sum1]

    mids, top_own = top_prepare(where, skel_top, pairs)
    tops = [top_own]
    for distance in range(1, groups):
        tops.append(swapped(top_own, "leaf", groups, distance))

    for at, span in enumerate((first + second, third, inner, last)):
        stage = "first" if at == 0 else "middle"
        part = [got[distance] for distance in span]
        sums = [near_remote(pool, near_count, blocks, tsq, span[0], part, sums, stage)]
    total = far(
        where, mid_partners, mids, sums[0], tops, interp_top[0], interp_mid[0], leaf_interpolant
    )
    return total.T


def solution(mesh):
    placed = (
        P(("leaf", "sub"), None),
        P(("leaf", "sub"), None),
        P(("leaf", "sub"), None),
        P(("leaf", "sub"), None, None),
        P(("leaf", "sub"), None),
        P(("leaf", "sub"), None, None),
        P(("leaf", "sub"), None),
        P(("leaf", "sub"), None),
        P("leaf", "sub", None),
        P("leaf", None),
    )
    return jax.shard_map(
        body, mesh=mesh, in_specs=placed, out_specs=P(("leaf", "sub"), None), check_vma=False
    )
```

```python
import functools
import math

import jax
import jax.numpy as jnp
from jax import lax
from jax.experimental import pallas as pl
from jax.experimental.pallas import tpu as pltpu
from jax.sharding import PartitionSpec as P


CAP = 2
UNROLL = 4
LANES = 128
kernel_rate = 0.25
VMEM_BYTES = 67043328
LOG2E = math.log2(math.e)
bf16 = jnp.bfloat16
f32 = jnp.float32
i32 = jnp.int32

ROWS_ROWS = (((1,), (1,)), ((), ()))


def dot(a, b):
    return jnp.dot(a, b, preferred_element_type=f32)


def dot_rows(a, b):
    return lax.dot_general(a, b, ROWS_ROWS, preferred_element_type=f32)


def squares(x):
    xf = x.astype(f32)
    sq = xf * xf
    high = sq.astype(bf16)
    low = (sq - high.astype(f32)).astype(bf16)
    return jnp.concatenate((high, low), axis=1)


def source_term(x):
    xf = x.astype(f32)
    total = jnp.sum(xf * xf, axis=1, keepdims=True) * (-kernel_rate * LOG2E)
    return jnp.broadcast_to(total, (x.shape[0], LANES))


def target_term(x):
    ones = jnp.ones((8, 2 * x.shape[1]), bf16)
    return dot_rows(ones, squares(x)) * (-kernel_rate * LOG2E)


def kernel_tile(source, source_sq, target, target_sq):
    products = dot_rows(source, target)
    columns = []
    for at in range(0, target.shape[0], LANES):
        exponent = products[:, at : at + LANES] * (2.0 * kernel_rate * LOG2E) + (
            source_sq + target_sq[0:1, at : at + LANES]
        )
        columns.append(jnp.exp2(exponent).astype(bf16))
    return jnp.concatenate(columns, axis=1)


def cost(flops, bytes_accessed, transcendentals=0):
    return pl.CostEstimate(
        flops=int(flops), bytes_accessed=int(bytes_accessed), transcendentals=int(transcendentals)
    )


def room(shapes):
    total = 0
    for shape in shapes:
        count = shape.dtype.itemsize * math.prod(shape.shape[:-1])
        total += count * -(-shape.shape[-1] // LANES) * LANES
    return total


def in_hbm():
    return pl.BlockSpec(memory_space=pltpu.HBM)


def copy_in(source, target, sem):
    made = pltpu.make_async_copy(source, target, sem)
    made.start()
    return made


def call(kernel, out_shape, in_specs, estimate, operands, scratch=(), own=0, outs=None, alias=None):
    several = isinstance(out_shape, (tuple, list))
    shapes = out_shape if several else [out_shape]
    specs = outs or [vmem()] * len(shapes)
    grant = room(operands) + room(shapes) + own + (2 << 20) if own is not None else VMEM_BYTES
    return pl.pallas_call(
        kernel,
        out_shape=out_shape,
        in_specs=in_specs,
        out_specs=specs if several else specs[0],
        scratch_shapes=list(scratch),
        input_output_aliases=alias or {},
        compiler_params=pltpu.CompilerParams(vmem_limit_bytes=grant),
        cost_estimate=estimate,
    )(*operands)


def vmem():
    return pl.BlockSpec(memory_space=pltpu.VMEM)


def smem():
    return pl.BlockSpec(memory_space=pltpu.SMEM)


def want_kernel(leaf_dev, group, where, near, chosen, pool):
    base, self_index = where[0], where[1]
    rows, near_count = near.shape
    width = max(LANES, group * leaf_dev)
    local = near[...] - base
    lane = lax.broadcasted_iota(i32, (rows, width), 1)
    member = lax.rem(lane, leaf_dev)
    owner = lax.div(lane, leaf_dev)
    named = jnp.zeros((rows, width), f32)
    for entry in range(near_count):
        named = jnp.maximum(named, (local[:, entry : entry + 1] == lane).astype(f32))
    wanted = jnp.max(named, axis=0, keepdims=True)
    wanted = jnp.where(owner == self_index, 0.0, jnp.broadcast_to(wanted, (rows, width)))
    row_id = lax.broadcasted_iota(i32, (width, width), 0)
    col_id = lax.broadcasted_iota(i32, (width, width), 1)
    before = (lax.div(row_id, leaf_dev) == lax.div(col_id, leaf_dev)) & (row_id < col_id)
    rank = dot(wanted.astype(bf16), before.astype(f32).astype(bf16))
    slot = lax.broadcasted_iota(i32, (rows, width), 0).astype(f32)
    picked = jnp.where((wanted > 0.0) & (rank == slot), member.astype(f32), 0.0)
    owner_row = lax.broadcasted_iota(i32, (group, width), 0)
    owner_of = lax.div(lax.broadcasted_iota(i32, (group, width), 1), leaf_dev)
    belongs = (owner_row == owner_of).astype(f32).astype(bf16)
    chosen[...] = dot_rows(belongs, picked.astype(bf16)).astype(i32)
    place = jnp.zeros((rows, LANES), i32)
    short_lane = lax.broadcasted_iota(i32, (rows, LANES), 1)
    for entry in range(near_count):
        ids = local[:, entry : entry + 1]
        at = jnp.sum(jnp.where(ids == lane, rank, 0.0), axis=1, keepdims=True).astype(i32)
        distance = jnp.bitwise_xor(lax.div(ids, leaf_dev), self_index)
        index = jnp.where(
            distance == 0,
            lax.rem(ids, leaf_dev),
            leaf_dev + distance * CAP + jnp.clip(at, 0, CAP - 1),
        )
        place = jnp.where(short_lane == entry, index, place)
    pool[...] = place


def want(near_leaves, where, leaf_dev, group):
    rows = near_leaves.shape[0]
    return call(
        functools.partial(want_kernel, leaf_dev, group),
        [jax.ShapeDtypeStruct((group, rows), i32), jax.ShapeDtypeStruct((rows, LANES), i32)],
        [smem(), vmem()],
        cost(1e6, 1e5),
        (where, near_leaves),
        own=None,
    )


def pack_kernel(leaf_size, distances, count, where, handed, points, charges, *refs):
    blocks, refs = refs[:count], refs[count:]
    outs, refs = refs[: len(distances)], refs[len(distances) :]
    if count:
        pair, refs = refs[0], refs[1:]
    x, q, mid, sem_x, sem_q, sem_m, sem_out = refs
    self_index = where[1]
    rhs = charges.shape[0]
    rows = leaf_size + leaf_size // LANES * rhs
    taken, given = [], []
    mid_copies = [copy_in(block, mid.at[at], sem_m.at[at]) for at, block in enumerate(blocks)]
    for at, distance in enumerate(distances):
        peer = jnp.bitwise_xor(self_index, distance)
        for slot in range(CAP):
            leaf = handed[peer, slot]
            lanes = pl.ds(pl.multiple_of(leaf * leaf_size, leaf_size), leaf_size)
            put = at * CAP + slot
            taken.append(
                (
                    copy_in(points.at[leaf], x.at[put], sem_x.at[put]),
                    copy_in(charges.at[:, lanes], q.at[put], sem_q.at[put]),
                )
            )
    for at, waited in enumerate(mid_copies):
        waited.wait()
        to = pair.at[at * mid.shape[1] : (at + 1) * mid.shape[1], :]
        given.append(copy_in(mid.at[at], to, sem_m.at[at]))
    tiles = leaf_size // LANES
    for at, out in enumerate(outs):
        for slot in range(CAP):
            put = at * CAP + slot
            base = slot * rows
            taken[put][0].wait()
            given.append(
                copy_in(x.at[put], out.at[base : base + leaf_size, :], sem_out.at[put, 0])
            )
            taken[put][1].wait()
            for tile in range(tiles):
                row = base + leaf_size + tile * rhs
                lanes = pl.ds(tile * LANES, LANES)
                given.append(
                    copy_in(
                        q.at[put, :, lanes], out.at[row : row + rhs, :], sem_out.at[put, 1 + tile]
                    )
                )
    for one in given:
        one.wait()


def pack(where, handed, points, charges, distances, *blocks):
    _, leaf_size, coords = points.shape
    rhs = charges.shape[0]
    rows = CAP * (leaf_size + leaf_size // LANES * rhs)
    each = blocks[0].shape[0] if blocks else 16
    shapes = [(rows, coords) for _ in distances]
    if blocks:
        shapes.append((len(blocks) * each, coords))
    places = len(distances) * CAP
    sem = pltpu.SemaphoreType.DMA
    return call(
        functools.partial(pack_kernel, leaf_size, distances, len(blocks)),
        [jax.ShapeDtypeStruct(shape, bf16) for shape in shapes],
        [smem(), smem()] + [in_hbm()] * (2 + len(blocks)),
        cost(1e5, 2 * len(distances) * rows * coords * 2),
        (where, handed, points, charges) + blocks,
        scratch=[
            pltpu.VMEM((places, leaf_size, coords), bf16),
            pltpu.VMEM((places, rhs, leaf_size), bf16),
            pltpu.VMEM((max(len(blocks), 1), each, coords), bf16),
            sem((places,)),
            sem((places,)),
            sem((max(len(blocks), 1),)),
            sem((places, 1 + leaf_size // LANES)),
        ],
        own=None,
        outs=[in_hbm()] * len(shapes),
    )


def run_pairs(pool, near_count, leaves, keep, tl, sl, tile_of, charge_of, acc, base):
    def scan(leaf, count):
        for entry in range(near_count):
            kept, source = keep(pool[leaf, entry])
            tl[count] = leaf
            sl[count] = source
            count = count + kept.astype(i32)
        return count

    count = lax.fori_loop(leaves[0], leaves[1], scan, jnp.int32(0))

    def one(at):
        target, source = tl[at], sl[at]
        acc[target - base] += dot(charge_of(source), tile_of(target, source))

    def several(step, carry):
        for k in range(UNROLL):
            one(step * UNROLL + k)
        return carry

    def single(at, carry):
        one(at)
        return carry

    whole = lax.div(count, UNROLL)
    lax.fori_loop(0, whole, several, 0)
    lax.fori_loop(whole * UNROLL, count, single, 0)


def near_cost(pairs, leaf_size, coords, rhs):
    return cost(
        pairs * 2 * leaf_size * leaf_size * 4 * (coords + rhs), 3e6, pairs * leaf_size * leaf_size
    )


def near_local_kernel(near_count, leaves, pool, points, charges, *refs):
    if leaves[0] == 0:
        out, tsq, tl, sl, x, q, ssq, acc, sem_x, sem_q, sem_out = refs
    else:
        tsq, out, tl, sl, x, q, ssq, acc, sem_x, sem_q, sem_out = refs
    leaf_dev, leaf_size, _ = points.shape
    q_copy = copy_in(charges, q, sem_q)
    x_copies = [copy_in(points.at[m], x.at[m], sem_x.at[m]) for m in range(leaf_dev)]
    acc[...] = jnp.zeros_like(acc)
    for leaf, waited in enumerate(x_copies):
        waited.wait()
        ssq[leaf] = source_term(x[leaf])
        if leaves[0] == 0:
            tsq[leaf] = target_term(x[leaf])
    q_copy.wait()

    def charge_of(source):
        at = pl.multiple_of(source * leaf_size, leaf_size)
        return q[:, pl.ds(at, leaf_size)]

    def tile_of(target, source):
        return kernel_tile(x[source], ssq[source], x[target], tsq[target])

    def keep(index):
        return index < leaf_dev, index

    run_pairs(pool, near_count, leaves, keep, tl, sl, tile_of, charge_of, acc, leaves[0])
    copy_in(acc, out, sem_out).wait()


def near_local(pool, near_count, points, charges, leaves, *tsq):
    leaf_dev, leaf_size, coords = points.shape
    rhs = charges.shape[0]
    span = leaves[1] - leaves[0]
    result = jax.ShapeDtypeStruct((span, rhs, leaf_size), f32)
    terms = jax.ShapeDtypeStruct((leaf_dev, 8, leaf_size), f32)
    return call(
        functools.partial(near_local_kernel, near_count, leaves),
        result if tsq else [result, terms],
        [smem(), in_hbm(), in_hbm()] + [vmem()] * len(tsq),
        near_cost(span * near_count / 2, leaf_size, coords, rhs),
        (pool, points, charges) + tsq,
        scratch=[
            pltpu.SMEM((leaf_dev * near_count + 1,), i32),
            pltpu.SMEM((leaf_dev * near_count + 1,), i32),
            pltpu.VMEM(points.shape, bf16),
            pltpu.VMEM(charges.shape, bf16),
            pltpu.VMEM((leaf_dev, leaf_size, LANES), f32),
            pltpu.VMEM((span, rhs, leaf_size), f32),
            pltpu.SemaphoreType.DMA((leaf_dev,)),
            pltpu.SemaphoreType.DMA,
            pltpu.SemaphoreType.DMA,
        ],
        own=None,
        outs=[in_hbm()] if tsq else [in_hbm(), vmem()],
    )


def near_remote_kernel(near_count, first, parts, pool, points, tsq, *refs):
    got, refs = refs[:parts], refs[parts:]
    init, out, tl, sl, x, pts, ssq, qs, acc, sem_got, sem_x, sem_acc = refs
    leaf_dev, leaf_size, _ = points.shape
    rhs = acc.shape[1]
    tiles = leaf_size // LANES

    moves = []
    for part, message in enumerate(got):
        for slot in range(CAP):
            at = part * CAP + slot
            base = slot * (leaf_size + tiles * rhs)
            one = [copy_in(message.at[base : base + leaf_size, :], pts.at[at], sem_got.at[at, 0])]
            for tile in range(tiles):
                row = base + leaf_size + tile * rhs
                lanes = pl.ds(tile * LANES, LANES)
                one.append(
                    copy_in(
                        message.at[row : row + rhs, :], qs.at[at, :, lanes], sem_got.at[at, 1 + tile]
                    )
                )
            moves.append(one)
    x_copy = copy_in(points, x, sem_x)
    acc_copy = copy_in(init, acc, sem_acc)
    for at, one in enumerate(moves):
        one[0].wait()
        ssq[at] = source_term(pts[at])
        for move in one[1:]:
            move.wait()
    x_copy.wait()
    acc_copy.wait()

    low = leaf_dev + first * CAP

    def keep(index):
        return (index >= low) & (index < low + parts * CAP), index - low

    def tile_of(target, source):
        return kernel_tile(pts[source], ssq[source], x[target], tsq[target])

    run_pairs(pool, near_count, (0, leaf_dev), keep, tl, sl, tile_of, lambda s: qs[s], acc, 0)
    copy_in(acc, out, sem_acc).wait()


def near_remote(pool, near_count, points, tsq, first, got, init):
    leaf_dev, leaf_size, coords = points.shape
    rhs = init.shape[1]
    places = len(got) * CAP
    sem = pltpu.SemaphoreType.DMA
    return call(
        functools.partial(near_remote_kernel, near_count, first, len(got)),
        jax.ShapeDtypeStruct(init.shape, f32),
        [smem(), in_hbm(), vmem()] + [in_hbm()] * (len(got) + 1),
        near_cost(len(got) * leaf_dev, leaf_size, coords, rhs),
        (pool, points, tsq, *got, init),
        scratch=[
            pltpu.SMEM((leaf_dev * near_count + 1,), i32),
            pltpu.SMEM((leaf_dev * near_count + 1,), i32),
            pltpu.VMEM(points.shape, bf16),
            pltpu.VMEM((places, leaf_size, coords), bf16),
            pltpu.VMEM((places, leaf_size, LANES), f32),
            pltpu.VMEM((places, rhs, leaf_size), bf16),
            pltpu.VMEM(init.shape, f32),
            sem((places, 1 + leaf_size // LANES)),
            sem,
            sem,
        ],
        own=None,
        outs=[in_hbm()],
        alias={3 + len(got): 0},
    )


def store_halves(out, row, value):
    for tile in range(value.shape[1] // LANES):
        out[row : row + value.shape[0], :] = value[:, tile * LANES : (tile + 1) * LANES]
        row += value.shape[0]
    return row


def load_halves(ref, row, rows, width):
    tiles = [ref[row + t * rows : row + (t + 1) * rows, :] for t in range(width // LANES)]
    return jnp.concatenate(tiles, axis=1)


def skeleton_rows(skel_leaf, skel_mid, leaf_size):
    leaf_dev, skel = skel_leaf.shape
    column = lax.rem(skel_mid, skel)
    leaf = lax.div(skel_mid, skel)
    hit = lax.broadcasted_iota(i32, (skel, skel), 0) == column
    table = jnp.concatenate((lax.div(skel_leaf, 16), lax.rem(skel_leaf, 16)), axis=0)
    found = dot(table.astype(f32).astype(bf16), hit.astype(f32).astype(bf16))
    index = (found[:leaf_dev] * 16.0 + found[leaf_dev:]).astype(i32)
    row = lax.broadcasted_iota(i32, (leaf_dev, skel), 0)
    return jnp.sum(jnp.where(row == leaf, index + row * leaf_size, 0), axis=0, keepdims=True)


def as_column(row):
    return jnp.broadcast_to(row.astype(f32), (LANES, row.shape[1])).T.astype(i32)


def pick_rows(index, base, block):
    lane = lax.broadcasted_iota(i32, index.shape, 1)
    tiles = [
        (index == lane + (base + at)).astype(f32).astype(bf16)
        for at in range(0, block.shape[0], LANES)
    ]
    return dot(jnp.concatenate(tiles, axis=1), block)


def up_kernel(*refs):
    points, charges, leaf_interp, interp_mid, interp_top, skel_leaf, skel_mid, out = refs[:8]
    x, q, leaf_w, mid_w, top_w, sem_x, sem_l, sem_m, sem_q, sem_t = refs[8:]
    leaf_dev, leaf_size, skel = leaf_interp.shape
    leaves = range(leaf_dev)
    x_copies = [copy_in(points.at[m], x.at[m], sem_x.at[m]) for m in leaves]
    q_copy = copy_in(charges, q, sem_q)
    l_copies, m_copies = [], []
    for m in leaves:
        rows = pl.ds(m * skel, skel)
        l_copies.append(copy_in(leaf_interp.at[m], leaf_w.at[m], sem_l.at[m]))
        m_copies.append(copy_in(interp_mid.at[rows], mid_w.at[rows], sem_m.at[m]))
    t_copy = copy_in(interp_top, top_w, sem_t)

    rows = as_column(skeleton_rows(skel_leaf[...], skel_mid[...], leaf_size))
    picked = jnp.zeros((skel, x.shape[2]), f32)
    for m in leaves:
        x_copies[m].wait()
        picked = picked + pick_rows(rows, m * leaf_size, x[m])
    out[:skel, :] = picked.astype(bf16)
    total = jnp.zeros((q.shape[0], skel), f32)
    q_copy.wait()
    for m in leaves:
        l_copies[m].wait()
        leaf_up = dot(q[:, m * leaf_size : (m + 1) * leaf_size], leaf_w[m]).astype(bf16)
        m_copies[m].wait()
        total = total + dot(leaf_up, mid_w[m * skel : (m + 1) * skel, :])
    mid_up = total.astype(bf16)
    t_copy.wait()
    top = dot(mid_up, top_w[...])
    row = store_halves(out, skel, mid_up)
    store_halves(out, row, top.astype(bf16))


def up(points, charges, leaf_interp, interp_mid, interp_top, skel_leaf, skel_mid):
    leaf_dev, _, skel = leaf_interp.shape
    rhs = charges.shape[0]
    rows = skel + 2 * rhs * (skel // LANES)
    sem = pltpu.SemaphoreType.DMA
    whole = (points, charges, leaf_interp, interp_mid, interp_top)
    return call(
        up_kernel,
        jax.ShapeDtypeStruct((rows, LANES), bf16),
        [in_hbm()] * 5 + [vmem()] * 2,
        cost(3e9, 5e6),
        whole + (skel_leaf, skel_mid),
        scratch=[pltpu.VMEM(a.shape, bf16) for a in whole]
        + [sem((leaf_dev,)), sem((leaf_dev,)), sem((leaf_dev,)), sem, sem],
        own=None,
    )


def place(distance, size):
    half = size // 2
    return lax.rem(distance, half) * 2 + lax.div(distance, half)


def top_kernel(where, skel_top, *refs):
    pairs, (mids, out, sem) = refs[:-3], refs[-3:]
    size, rows, _ = mids.shape
    skel = skel_top.shape[1]
    copies = []
    for to in range(size):
        row = to % 2 * rows
        source = pairs[to // 2].at[row : row + rows, :]
        copies.append(copy_in(source, mids.at[to], sem.at[to]))
    picked = skel_top[...]
    distance = jnp.bitwise_xor(lax.div(picked, skel), where[1])
    index = as_column(place(distance, size) * skel + lax.rem(picked, skel))
    points = jnp.zeros((skel, mids.shape[2]), f32)
    first = skel + (rows - skel) // 2
    weight = jnp.zeros((rows - first, mids.shape[2]), f32)
    for p in range(size):
        copies[p].wait()
        points = points + pick_rows(index, p * skel, mids[p, :skel, :])
        weight = weight + mids[p, first:, :].astype(f32)
    out[:skel, :] = points.astype(bf16)
    out[skel:, :] = weight.astype(bf16)


def top_prepare(where, skel_top, pairs):
    rows, coords = pairs[0].shape[0] // 2, pairs[0].shape[1]
    skel = skel_top.shape[1]
    size = 2 * len(pairs)
    return call(
        top_kernel,
        [
            jax.ShapeDtypeStruct((size, rows, coords), bf16),
            jax.ShapeDtypeStruct((skel + (rows - skel) // 2, coords), bf16),
        ],
        [smem(), vmem()] + [in_hbm()] * len(pairs),
        cost(1e9, 2e6),
        (where, skel_top, *pairs),
        scratch=[pltpu.SemaphoreType.DMA((size,))],
        own=None,
    )


def far_kernel(where, partners, mids_in, acc, interp_top, mid_in, leaf_in, *refs):
    tops, refs = refs[:-9], refs[-9:]
    out, mids, sums, interp_mid, leaf_interp, sem_p, sem_a, sem_m, sem_l = refs
    leaf_dev, leaf_size, skel = leaf_interp.shape
    rhs = acc.shape[1]
    p_copy = copy_in(mids_in, mids, sem_p)
    m_copy = copy_in(mid_in, interp_mid, sem_m)
    l_copies = [copy_in(leaf_in.at[m], leaf_interp.at[m], sem_l.at[m]) for m in range(leaf_dev)]
    a_copy = copy_in(acc, sums, sem_a)

    def pair(source_ref, target, target_sq):
        source = source_ref[:skel, :]
        weight = load_halves(source_ref, skel, rhs, skel)
        tile = kernel_tile(source, source_term(source), target, target_sq)
        return dot(weight, tile)

    target = tops[0][:skel, :]
    target_sq = target_term(target)
    top_sum = jnp.zeros((rhs, skel), f32)
    for other in tops[1:]:
        top_sum = top_sum + pair(other, target, target_sq)
    p_copy.wait()
    target = mids[0, :skel, :]
    target_sq = target_term(target)
    mid_sum = jnp.zeros((rhs, skel), f32)
    for at in range(partners.shape[1]):
        distance = jnp.bitwise_xor(partners[0, at] - where[2], where[1])
        mid_sum = mid_sum + pair(mids.at[place(distance, mids.shape[0])], target, target_sq)
    total = (mid_sum + dot_rows(top_sum.astype(bf16), interp_top[...])).astype(bf16)
    m_copy.wait()
    for m in range(leaf_dev):
        leaf_down = dot_rows(total, interp_mid[m * skel : (m + 1) * skel, :]).astype(bf16)
        l_copies[m].wait()
        distant = dot_rows(leaf_down, leaf_interp[m])
        if m == 0:
            a_copy.wait()
        out[:, m * leaf_size : (m + 1) * leaf_size] = sums[m] + distant


def far(where, partners, mids, acc, tops, interp_top, interp_mid, leaf_interp):
    leaf_dev, leaf_size, _ = leaf_interp.shape
    rhs = acc.shape[1]
    return call(
        far_kernel,
        jax.ShapeDtypeStruct((rhs, leaf_dev * leaf_size), f32),
        [smem()] * 2 + [in_hbm()] * 2 + [vmem()] + [in_hbm()] * 2 + [vmem()] * len(tops),
        cost(1e9, 6e6, 5e5),
        (where, partners, mids, acc, interp_top, interp_mid, leaf_interp, *tops),
        scratch=[
            pltpu.VMEM(mids.shape, bf16),
            pltpu.VMEM(acc.shape, f32),
            pltpu.VMEM(interp_mid.shape, bf16),
            pltpu.VMEM(leaf_interp.shape, bf16),
            pltpu.SemaphoreType.DMA,
            pltpu.SemaphoreType.DMA,
            pltpu.SemaphoreType.DMA,
            pltpu.SemaphoreType.DMA((leaf_dev,)),
        ],
        own=None,
    )


def swapped(value, axis, size, distance):
    return lax.ppermute(value, axis, [(i, i ^ distance) for i in range(size)])


def across(group):
    half = group // 2
    cuts = [half, half + max(half // 4, 1), half + half // 2, half + half * 3 // 4, group]
    return [list(range(*cut)) for cut in zip(cuts, cuts[1:])]


def body(
    points,
    charges,
    near_leaves,
    leaf_interpolant,
    skel_leaf,
    interp_mid,
    skel_mid,
    mid_partners,
    interp_top,
    skel_top,
):
    group = lax.axis_size("sub")
    groups = lax.axis_size("leaf")
    self_index = lax.axis_index("sub")
    leaf_dev, leaf_size, _ = leaf_interpolant.shape
    coords = points.shape[1]
    near_count = near_leaves.shape[1]
    group_first = lax.axis_index("leaf") * group
    blocks = points.reshape(leaf_dev, leaf_size, coords)
    charges_t = charges.T

    where = jnp.stack((group_first * leaf_dev, self_index, group_first)).astype(i32)
    chosen, pool = want(near_leaves, where, leaf_dev, group)
    handed = lax.all_to_all(chosen, "sub", split_axis=0, concat_axis=0, tiled=True)

    message = up(
        blocks, charges_t, leaf_interpolant, interp_mid[0], interp_top[0], skel_leaf, skel_mid
    )
    across_message = swapped(message, "sub", group, group // 2)

    first, second, third, last = across(group)
    inner = list(range(1, group // 2))
    got = {}
    for distances, carried in ((first + second + third + last, ()), (inner, (message, across_message))):
        asked = pack(where, handed, blocks, charges_t, distances, *carried)
        for distance, one in zip(distances, asked):
            got[distance] = swapped(one, "sub", group, distance)
    pair = asked[-1]
    pairs = [pair] + [swapped(pair, "sub", group, d) for d in inner]

    local_sum, tsq = near_local(pool, near_count, blocks, charges_t, (0, leaf_dev))
    total = local_sum

    mids, top_own = top_prepare(where, skel_top, pairs)
    tops = [top_own]
    for distance in range(1, groups):
        tops.append(swapped(top_own, "leaf", groups, distance))

    for span in (first + second, inner, third, last):
        part = [got[distance] for distance in span]
        total = near_remote(pool, near_count, blocks, tsq, span[0], part, total)
    total = far(
        where, mid_partners, mids, total, tops, interp_top[0], interp_mid[0], leaf_interpolant
    )
    return total.T


def solution(mesh):
    placed = (
        P(("leaf", "sub"), None),
        P(("leaf", "sub"), None),
        P(("leaf", "sub"), None),
        P(("leaf", "sub"), None, None),
        P(("leaf", "sub"), None),
        P(("leaf", "sub"), None, None),
        P(("leaf", "sub"), None),
        P(("leaf", "sub"), None),
        P("leaf", "sub", None),
        P("leaf", None),
    )
    return jax.shard_map(
        body, mesh=mesh, in_specs=placed, out_specs=P(("leaf", "sub"), None), check_vma=False
    )
```

```python
import functools
import math

import jax
import jax.numpy as jnp
from jax import lax
from jax.experimental import pallas as pl
from jax.experimental.pallas import tpu as pltpu
from jax.sharding import PartitionSpec as P


CAP = 2
UNROLL = 4
LANES = 128
kernel_rate = 0.25
VMEM_BYTES = 67043328
LOG2E = math.log2(math.e)
bf16 = jnp.bfloat16
f32 = jnp.float32
i32 = jnp.int32

ROWS_ROWS = (((1,), (1,)), ((), ()))


def dot(a, b):
    return jnp.dot(a, b, preferred_element_type=f32)


def dot_rows(a, b):
    return lax.dot_general(a, b, ROWS_ROWS, preferred_element_type=f32)


def squares(x):
    xf = x.astype(f32)
    sq = xf * xf
    high = sq.astype(bf16)
    low = (sq - high.astype(f32)).astype(bf16)
    return jnp.concatenate((high, low), axis=1)


def source_term(x):
    xf = x.astype(f32)
    total = jnp.sum(xf * xf, axis=1, keepdims=True) * (-kernel_rate * LOG2E)
    return jnp.broadcast_to(total, (x.shape[0], LANES))


def target_term(x):
    ones = jnp.ones((8, 2 * x.shape[1]), bf16)
    return dot_rows(ones, squares(x)) * (-kernel_rate * LOG2E)


def kernel_tile(source, source_sq, target, target_sq):
    products = dot_rows(source, target)
    columns = []
    for at in range(0, target.shape[0], LANES):
        exponent = products[:, at : at + LANES] * (2.0 * kernel_rate * LOG2E) + (
            source_sq + target_sq[0:1, at : at + LANES]
        )
        columns.append(jnp.exp2(exponent).astype(bf16))
    return jnp.concatenate(columns, axis=1)


def cost(flops, bytes_accessed, transcendentals=0):
    return pl.CostEstimate(
        flops=int(flops), bytes_accessed=int(bytes_accessed), transcendentals=int(transcendentals)
    )


def room(shapes):
    total = 0
    for shape in shapes:
        count = shape.dtype.itemsize * math.prod(shape.shape[:-1])
        total += count * -(-shape.shape[-1] // LANES) * LANES
    return total


def in_hbm():
    return pl.BlockSpec(memory_space=pltpu.HBM)


def copy_in(source, target, sem):
    made = pltpu.make_async_copy(source, target, sem)
    made.start()
    return made


def call(kernel, out_shape, in_specs, estimate, operands, scratch=(), own=0, outs=None, alias=None):
    several = isinstance(out_shape, (tuple, list))
    shapes = out_shape if several else [out_shape]
    specs = outs or [vmem()] * len(shapes)
    grant = room(operands) + room(shapes) + own + (2 << 20) if own is not None else VMEM_BYTES
    return pl.pallas_call(
        kernel,
        out_shape=out_shape,
        in_specs=in_specs,
        out_specs=specs if several else specs[0],
        scratch_shapes=list(scratch),
        input_output_aliases=alias or {},
        compiler_params=pltpu.CompilerParams(vmem_limit_bytes=grant),
        cost_estimate=estimate,
    )(*operands)


def vmem():
    return pl.BlockSpec(memory_space=pltpu.VMEM)


def smem():
    return pl.BlockSpec(memory_space=pltpu.SMEM)


def want_kernel(leaf_dev, group, where, near, chosen, pool):
    base, self_index = where[0], where[1]
    rows, near_count = near.shape
    width = max(LANES, group * leaf_dev)
    local = near[...] - base
    lane = lax.broadcasted_iota(i32, (rows, width), 1)
    member = lax.rem(lane, leaf_dev)
    owner = lax.div(lane, leaf_dev)
    named = jnp.zeros((rows, width), f32)
    for entry in range(near_count):
        named = jnp.maximum(named, (local[:, entry : entry + 1] == lane).astype(f32))
    wanted = jnp.max(named, axis=0, keepdims=True)
    wanted = jnp.where(owner == self_index, 0.0, jnp.broadcast_to(wanted, (rows, width)))
    row_id = lax.broadcasted_iota(i32, (width, width), 0)
    col_id = lax.broadcasted_iota(i32, (width, width), 1)
    before = (lax.div(row_id, leaf_dev) == lax.div(col_id, leaf_dev)) & (row_id < col_id)
    rank = dot(wanted.astype(bf16), before.astype(f32).astype(bf16))
    slot = lax.broadcasted_iota(i32, (rows, width), 0).astype(f32)
    picked = jnp.where((wanted > 0.0) & (rank == slot), member.astype(f32), 0.0)
    owner_row = lax.broadcasted_iota(i32, (group, width), 0)
    owner_of = lax.div(lax.broadcasted_iota(i32, (group, width), 1), leaf_dev)
    belongs = (owner_row == owner_of).astype(f32).astype(bf16)
    chosen[...] = dot_rows(belongs, picked.astype(bf16)).astype(i32)
    place = jnp.zeros((rows, LANES), i32)
    short_lane = lax.broadcasted_iota(i32, (rows, LANES), 1)
    for entry in range(near_count):
        ids = local[:, entry : entry + 1]
        at = jnp.sum(jnp.where(ids == lane, rank, 0.0), axis=1, keepdims=True).astype(i32)
        distance = jnp.bitwise_xor(lax.div(ids, leaf_dev), self_index)
        index = jnp.where(
            distance == 0,
            lax.rem(ids, leaf_dev),
            leaf_dev + distance * CAP + jnp.clip(at, 0, CAP - 1),
        )
        place = jnp.where(short_lane == entry, index, place)
    pool[...] = place


def want(near_leaves, where, leaf_dev, group):
    rows = near_leaves.shape[0]
    return call(
        functools.partial(want_kernel, leaf_dev, group),
        [jax.ShapeDtypeStruct((group, rows), i32), jax.ShapeDtypeStruct((rows, LANES), i32)],
        [smem(), vmem()],
        cost(1e6, 1e5),
        (where, near_leaves),
        own=None,
    )


def pack_kernel(leaf_size, distances, count, where, handed, points, charges, *refs):
    blocks, refs = refs[:count], refs[count:]
    outs, refs = refs[: len(distances)], refs[len(distances) :]
    if count:
        pair, refs = refs[0], refs[1:]
    x, q, mid, sem_x, sem_q, sem_m, sem_out = refs
    self_index = where[1]
    rhs = charges.shape[0]
    rows = leaf_size + leaf_size // LANES * rhs
    taken, given = [], []
    mid_copies = [copy_in(block, mid.at[at], sem_m.at[at]) for at, block in enumerate(blocks)]
    for at, distance in enumerate(distances):
        peer = jnp.bitwise_xor(self_index, distance)
        for slot in range(CAP):
            leaf = handed[peer, slot]
            lanes = pl.ds(pl.multiple_of(leaf * leaf_size, leaf_size), leaf_size)
            put = at * CAP + slot
            taken.append(
                (
                    copy_in(points.at[leaf], x.at[put], sem_x.at[put]),
                    copy_in(charges.at[:, lanes], q.at[put], sem_q.at[put]),
                )
            )
    for at, waited in enumerate(mid_copies):
        waited.wait()
        to = pair.at[at * mid.shape[1] : (at + 1) * mid.shape[1], :]
        given.append(copy_in(mid.at[at], to, sem_m.at[at]))
    tiles = leaf_size // LANES
    for at, out in enumerate(outs):
        for slot in range(CAP):
            put = at * CAP + slot
            base = slot * rows
            taken[put][0].wait()
            given.append(
                copy_in(x.at[put], out.at[base : base + leaf_size, :], sem_out.at[put, 0])
            )
            taken[put][1].wait()
            for tile in range(tiles):
                row = base + leaf_size + tile * rhs
                lanes = pl.ds(tile * LANES, LANES)
                given.append(
                    copy_in(
                        q.at[put, :, lanes], out.at[row : row + rhs, :], sem_out.at[put, 1 + tile]
                    )
                )
    for one in given:
        one.wait()


def pack(where, handed, points, charges, distances, *blocks):
    _, leaf_size, coords = points.shape
    rhs = charges.shape[0]
    rows = CAP * (leaf_size + leaf_size // LANES * rhs)
    each = blocks[0].shape[0] if blocks else 16
    shapes = [(rows, coords) for _ in distances]
    if blocks:
        shapes.append((len(blocks) * each, coords))
    places = len(distances) * CAP
    sem = pltpu.SemaphoreType.DMA
    return call(
        functools.partial(pack_kernel, leaf_size, distances, len(blocks)),
        [jax.ShapeDtypeStruct(shape, bf16) for shape in shapes],
        [smem(), smem()] + [in_hbm()] * (2 + len(blocks)),
        cost(1e5, 2 * len(distances) * rows * coords * 2),
        (where, handed, points, charges) + blocks,
        scratch=[
            pltpu.VMEM((places, leaf_size, coords), bf16),
            pltpu.VMEM((places, rhs, leaf_size), bf16),
            pltpu.VMEM((max(len(blocks), 1), each, coords), bf16),
            sem((places,)),
            sem((places,)),
            sem((max(len(blocks), 1),)),
            sem((places, 1 + leaf_size // LANES)),
        ],
        own=None,
        outs=[in_hbm()] * len(shapes),
    )


def run_pairs(pool, near_count, leaves, keep, tl, sl, tile_of, charge_of, acc, base):
    def scan(leaf, count):
        for entry in range(near_count):
            kept, source = keep(pool[leaf, entry])
            tl[count] = leaf
            sl[count] = source
            count = count + kept.astype(i32)
        return count

    count = lax.fori_loop(leaves[0], leaves[1], scan, jnp.int32(0))

    def one(at):
        target, source = tl[at], sl[at]
        acc[target - base] += dot(charge_of(source), tile_of(target, source))

    def several(step, carry):
        for k in range(UNROLL):
            one(step * UNROLL + k)
        return carry

    def single(at, carry):
        one(at)
        return carry

    whole = lax.div(count, UNROLL)
    lax.fori_loop(0, whole, several, 0)
    lax.fori_loop(whole * UNROLL, count, single, 0)


def near_cost(pairs, leaf_size, coords, rhs):
    return cost(
        pairs * 2 * leaf_size * leaf_size * 4 * (coords + rhs), 3e6, pairs * leaf_size * leaf_size
    )


def near_local_kernel(near_count, leaves, pool, points, charges, *refs):
    if leaves[0] == 0:
        out, tsq, tl, sl, x, q, ssq, acc, sem_x, sem_q, sem_out = refs
    else:
        tsq, out, tl, sl, x, q, ssq, acc, sem_x, sem_q, sem_out = refs
    leaf_dev, leaf_size, _ = points.shape
    q_copy = copy_in(charges, q, sem_q)
    x_copies = [copy_in(points.at[m], x.at[m], sem_x.at[m]) for m in range(leaf_dev)]
    acc[...] = jnp.zeros_like(acc)
    for leaf, waited in enumerate(x_copies):
        waited.wait()
        ssq[leaf] = source_term(x[leaf])
        if leaves[0] == 0:
            tsq[leaf] = target_term(x[leaf])
    q_copy.wait()

    def charge_of(source):
        at = pl.multiple_of(source * leaf_size, leaf_size)
        return q[:, pl.ds(at, leaf_size)]

    def tile_of(target, source):
        return kernel_tile(x[source], ssq[source], x[target], tsq[target])

    def keep(index):
        return index < leaf_dev, index

    run_pairs(pool, near_count, leaves, keep, tl, sl, tile_of, charge_of, acc, leaves[0])
    copy_in(acc, out, sem_out).wait()


def near_local(pool, near_count, points, charges, leaves, *tsq):
    leaf_dev, leaf_size, coords = points.shape
    rhs = charges.shape[0]
    span = leaves[1] - leaves[0]
    result = jax.ShapeDtypeStruct((span, rhs, leaf_size), f32)
    terms = jax.ShapeDtypeStruct((leaf_dev, 8, leaf_size), f32)
    return call(
        functools.partial(near_local_kernel, near_count, leaves),
        result if tsq else [result, terms],
        [smem(), in_hbm(), in_hbm()] + [vmem()] * len(tsq),
        near_cost(span * near_count / 2, leaf_size, coords, rhs),
        (pool, points, charges) + tsq,
        scratch=[
            pltpu.SMEM((leaf_dev * near_count + 1,), i32),
            pltpu.SMEM((leaf_dev * near_count + 1,), i32),
            pltpu.VMEM(points.shape, bf16),
            pltpu.VMEM(charges.shape, bf16),
            pltpu.VMEM((leaf_dev, leaf_size, LANES), f32),
            pltpu.VMEM((span, rhs, leaf_size), f32),
            pltpu.SemaphoreType.DMA((leaf_dev,)),
            pltpu.SemaphoreType.DMA,
            pltpu.SemaphoreType.DMA,
        ],
        own=None,
        outs=[in_hbm()] if tsq else [in_hbm(), vmem()],
    )


def near_remote_kernel(near_count, first, parts, stage, pool, points, tsq, *refs):
    got, refs = refs[:parts], refs[parts:]
    taken = 2 if stage == "first" else 1
    inits, refs = refs[:taken], refs[taken:]
    acc, tl, sl, x, pts, ssq, qs, sem_got, sem_x, sem_acc = refs
    leaf_dev, leaf_size, _ = points.shape
    rhs = acc.shape[1]
    tiles = leaf_size // LANES

    moves = []
    for part, message in enumerate(got):
        for slot in range(CAP):
            at = part * CAP + slot
            base = slot * (leaf_size + tiles * rhs)
            one = [copy_in(message.at[base : base + leaf_size, :], pts.at[at], sem_got.at[at, 0])]
            for tile in range(tiles):
                row = base + leaf_size + tile * rhs
                lanes = pl.ds(tile * LANES, LANES)
                one.append(
                    copy_in(
                        message.at[row : row + rhs, :], qs.at[at, :, lanes], sem_got.at[at, 1 + tile]
                    )
                )
            moves.append(one)
    x_copy = copy_in(points, x, sem_x)
    acc_copies = []
    if stage == "first":
        base = 0
        for at, init in enumerate(inits):
            rows = pl.ds(base, init.shape[0])
            acc_copies.append(copy_in(init, acc.at[rows], sem_acc.at[at]))
            base += init.shape[0]
    for at, one in enumerate(moves):
        one[0].wait()
        ssq[at] = source_term(pts[at])
        for move in one[1:]:
            move.wait()
    x_copy.wait()
    for move in acc_copies:
        move.wait()

    low = leaf_dev + first * CAP

    def keep(index):
        return (index >= low) & (index < low + parts * CAP), index - low

    def tile_of(target, source):
        return kernel_tile(pts[source], ssq[source], x[target], tsq[target])

    run_pairs(pool, near_count, (0, leaf_dev), keep, tl, sl, tile_of, lambda s: qs[s], acc, 0)


def near_remote(pool, near_count, points, tsq, first, got, inits, stage):
    leaf_dev, leaf_size, coords = points.shape
    rhs = inits[0].shape[1]
    places = len(got) * CAP
    sums = (leaf_dev, rhs, leaf_size)
    scratch = [
        pltpu.SMEM((leaf_dev * near_count + 1,), i32),
        pltpu.SMEM((leaf_dev * near_count + 1,), i32),
        pltpu.VMEM(points.shape, bf16),
        pltpu.VMEM((places, leaf_size, coords), bf16),
        pltpu.VMEM((places, leaf_size, LANES), f32),
        pltpu.VMEM((places, rhs, leaf_size), bf16),
        pltpu.SemaphoreType.DMA((places, 1 + leaf_size // LANES)),
        pltpu.SemaphoreType.DMA,
        pltpu.SemaphoreType.DMA((2,)),
    ]
    spec = in_hbm() if stage == "first" else vmem()
    return call(
        functools.partial(near_remote_kernel, near_count, first, len(got), stage),
        jax.ShapeDtypeStruct(sums, f32),
        [smem(), in_hbm(), vmem()] + [in_hbm()] * len(got) + [spec] * len(inits),
        near_cost(len(got) * leaf_dev, leaf_size, coords, rhs),
        (pool, points, tsq, *got, *inits),
        scratch=scratch,
        own=None
        if stage == "first"
        else (leaf_dev * rhs * 4 + places * (coords * 2 + LANES * 4 + rhs * 2)) * leaf_size
        + (2 << 20),
        alias={3 + len(got): 0} if stage == "middle" else None,
    )


def store_halves(out, row, value):
    for tile in range(value.shape[1] // LANES):
        out[row : row + value.shape[0], :] = value[:, tile * LANES : (tile + 1) * LANES]
        row += value.shape[0]
    return row


def load_halves(ref, row, rows, width):
    tiles = [ref[row + t * rows : row + (t + 1) * rows, :] for t in range(width // LANES)]
    return jnp.concatenate(tiles, axis=1)


def skeleton_rows(skel_leaf, skel_mid, leaf_size):
    leaf_dev, skel = skel_leaf.shape
    column = lax.rem(skel_mid, skel)
    leaf = lax.div(skel_mid, skel)
    hit = lax.broadcasted_iota(i32, (skel, skel), 0) == column
    table = jnp.concatenate((lax.div(skel_leaf, 16), lax.rem(skel_leaf, 16)), axis=0)
    found = dot(table.astype(f32).astype(bf16), hit.astype(f32).astype(bf16))
    index = (found[:leaf_dev] * 16.0 + found[leaf_dev:]).astype(i32)
    row = lax.broadcasted_iota(i32, (leaf_dev, skel), 0)
    return jnp.sum(jnp.where(row == leaf, index + row * leaf_size, 0), axis=0, keepdims=True)


def as_column(row):
    return jnp.broadcast_to(row.astype(f32), (LANES, row.shape[1])).T.astype(i32)


def pick_rows(index, base, block):
    lane = lax.broadcasted_iota(i32, index.shape, 1)
    tiles = [
        (index == lane + (base + at)).astype(f32).astype(bf16)
        for at in range(0, block.shape[0], LANES)
    ]
    return dot(jnp.concatenate(tiles, axis=1), block)


def up_kernel(*refs):
    points, charges, leaf_interp, interp_mid, interp_top, skel_leaf, skel_mid, out = refs[:8]
    x, q, leaf_w, mid_w, top_w, sem_x, sem_l, sem_m, sem_q, sem_t = refs[8:]
    leaf_dev, leaf_size, skel = leaf_interp.shape
    leaves = range(leaf_dev)
    x_copies = [copy_in(points.at[m], x.at[m], sem_x.at[m]) for m in leaves]
    q_copy = copy_in(charges, q, sem_q)
    l_copies, m_copies = [], []
    for m in leaves:
        rows = pl.ds(m * skel, skel)
        l_copies.append(copy_in(leaf_interp.at[m], leaf_w.at[m], sem_l.at[m]))
        m_copies.append(copy_in(interp_mid.at[rows], mid_w.at[rows], sem_m.at[m]))
    t_copy = copy_in(interp_top, top_w, sem_t)

    rows = as_column(skeleton_rows(skel_leaf[...], skel_mid[...], leaf_size))
    picked = jnp.zeros((skel, x.shape[2]), f32)
    for m in leaves:
        x_copies[m].wait()
        picked = picked + pick_rows(rows, m * leaf_size, x[m])
    out[:skel, :] = picked.astype(bf16)
    total = jnp.zeros((q.shape[0], skel), f32)
    q_copy.wait()
    for m in leaves:
        l_copies[m].wait()
        leaf_up = dot(q[:, m * leaf_size : (m + 1) * leaf_size], leaf_w[m]).astype(bf16)
        m_copies[m].wait()
        total = total + dot(leaf_up, mid_w[m * skel : (m + 1) * skel, :])
    mid_up = total.astype(bf16)
    t_copy.wait()
    top = dot(mid_up, top_w[...])
    row = store_halves(out, skel, mid_up)
    store_halves(out, row, top.astype(bf16))


def up(points, charges, leaf_interp, interp_mid, interp_top, skel_leaf, skel_mid):
    leaf_dev, _, skel = leaf_interp.shape
    rhs = charges.shape[0]
    rows = skel + 2 * rhs * (skel // LANES)
    sem = pltpu.SemaphoreType.DMA
    whole = (points, charges, leaf_interp, interp_mid, interp_top)
    return call(
        up_kernel,
        jax.ShapeDtypeStruct((rows, LANES), bf16),
        [in_hbm()] * 5 + [vmem()] * 2,
        cost(3e9, 5e6),
        whole + (skel_leaf, skel_mid),
        scratch=[pltpu.VMEM(a.shape, bf16) for a in whole]
        + [sem((leaf_dev,)), sem((leaf_dev,)), sem((leaf_dev,)), sem, sem],
        own=None,
    )


def place(distance, size):
    half = size // 2
    return lax.rem(distance, half) * 2 + lax.div(distance, half)


def top_kernel(where, skel_top, *refs):
    pairs, (mids, out, sem) = refs[:-3], refs[-3:]
    size, rows, _ = mids.shape
    skel = skel_top.shape[1]
    copies = []
    for to in range(size):
        row = to % 2 * rows
        source = pairs[to // 2].at[row : row + rows, :]
        copies.append(copy_in(source, mids.at[to], sem.at[to]))
    picked = skel_top[...]
    distance = jnp.bitwise_xor(lax.div(picked, skel), where[1])
    index = as_column(place(distance, size) * skel + lax.rem(picked, skel))
    points = jnp.zeros((skel, mids.shape[2]), f32)
    first = skel + (rows - skel) // 2
    weight = jnp.zeros((rows - first, mids.shape[2]), f32)
    for p in range(size):
        copies[p].wait()
        points = points + pick_rows(index, p * skel, mids[p, :skel, :])
        weight = weight + mids[p, first:, :].astype(f32)
    out[:skel, :] = points.astype(bf16)
    out[skel:, :] = weight.astype(bf16)


def top_prepare(where, skel_top, pairs):
    rows, coords = pairs[0].shape[0] // 2, pairs[0].shape[1]
    skel = skel_top.shape[1]
    size = 2 * len(pairs)
    return call(
        top_kernel,
        [
            jax.ShapeDtypeStruct((size, rows, coords), bf16),
            jax.ShapeDtypeStruct((skel + (rows - skel) // 2, coords), bf16),
        ],
        [smem(), vmem()] + [in_hbm()] * len(pairs),
        cost(1e9, 2e6),
        (where, skel_top, *pairs),
        scratch=[pltpu.SemaphoreType.DMA((size,))],
        own=2 << 20,
    )


def far_kernel(where, partners, mids, acc, interp_top, interp_mid, leaf_interp, *refs):
    tops, out = refs[:-1], refs[-1]
    leaf_dev, leaf_size, skel = leaf_interp.shape
    rhs = acc.shape[1]

    def pair(source_ref, target, target_sq):
        source = source_ref[:skel, :]
        weight = load_halves(source_ref, skel, rhs, skel)
        tile = kernel_tile(source, source_term(source), target, target_sq)
        return dot(weight, tile)

    target = tops[0][:skel, :]
    target_sq = target_term(target)
    top_sum = jnp.zeros((rhs, skel), f32)
    for other in tops[1:]:
        top_sum = top_sum + pair(other, target, target_sq)
    target = mids[0, :skel, :]
    target_sq = target_term(target)
    mid_sum = jnp.zeros((rhs, skel), f32)
    for at in range(partners.shape[1]):
        distance = jnp.bitwise_xor(partners[0, at] - where[2], where[1])
        mid_sum = mid_sum + pair(mids.at[place(distance, mids.shape[0])], target, target_sq)
    total = (mid_sum + dot_rows(top_sum.astype(bf16), interp_top[...])).astype(bf16)
    for m in range(leaf_dev):
        leaf_down = dot_rows(total, interp_mid[m * skel : (m + 1) * skel, :]).astype(bf16)
        distant = dot_rows(leaf_down, leaf_interp[m])
        out[:, m * leaf_size : (m + 1) * leaf_size] = acc[m] + distant


def far(where, partners, mids, acc, tops, interp_top, interp_mid, leaf_interp):
    leaf_dev, leaf_size, _ = leaf_interp.shape
    rhs = acc.shape[1]
    return call(
        far_kernel,
        jax.ShapeDtypeStruct((rhs, leaf_dev * leaf_size), f32),
        [smem()] * 2 + [vmem()] * (5 + len(tops)),
        cost(1e9, 6e6, 5e5),
        (where, partners, mids, acc, interp_top, interp_mid, leaf_interp, *tops),
        own=1 << 20,
    )


def swapped(value, axis, size, distance):
    return lax.ppermute(value, axis, [(i, i ^ distance) for i in range(size)])


def across(group):
    half = group // 2
    cuts = [half, half + max(half // 4, 1), half + half // 2, half + half * 3 // 4, group]
    return [list(range(*cut)) for cut in zip(cuts, cuts[1:])]


def body(
    points,
    charges,
    near_leaves,
    leaf_interpolant,
    skel_leaf,
    interp_mid,
    skel_mid,
    mid_partners,
    interp_top,
    skel_top,
):
    group = lax.axis_size("sub")
    groups = lax.axis_size("leaf")
    self_index = lax.axis_index("sub")
    leaf_dev, leaf_size, _ = leaf_interpolant.shape
    coords = points.shape[1]
    near_count = near_leaves.shape[1]
    group_first = lax.axis_index("leaf") * group
    blocks = points.reshape(leaf_dev, leaf_size, coords)
    charges_t = charges.T

    where = jnp.stack((group_first * leaf_dev, self_index, group_first)).astype(i32)
    chosen, pool = want(near_leaves, where, leaf_dev, group)
    handed = lax.all_to_all(chosen, "sub", split_axis=0, concat_axis=0, tiled=True)

    message = up(
        blocks, charges_t, leaf_interpolant, interp_mid[0], interp_top[0], skel_leaf, skel_mid
    )
    across_message = swapped(message, "sub", group, group // 2)

    first, second, third, last = across(group)
    inner = list(range(1, group // 2))
    got = {}
    for distances in (first + second + inner, third + last):
        asked = pack(where, handed, blocks, charges_t, distances)
        for distance, one in zip(distances, asked):
            got[distance] = swapped(one, "sub", group, distance)
    pair = jnp.concatenate((message, across_message), axis=0)
    pairs = [pair] + [swapped(pair, "sub", group, d) for d in inner]

    half = leaf_dev // 2
    sum0, tsq = near_local(pool, near_count, blocks, charges_t, (0, half))
    sum1 = near_local(pool, near_count, blocks, charges_t, (half, leaf_dev), tsq)
    sums = [sum0, sum1]

    mids, top_own = top_prepare(where, skel_top, pairs)
    tops = [top_own]
    for distance in range(1, groups):
        tops.append(swapped(top_own, "leaf", groups, distance))

    for at, span in enumerate((inner + first + second, third + last)):
        stage = "first" if at == 0 else "middle"
        part = [got[distance] for distance in span]
        sums = [near_remote(pool, near_count, blocks, tsq, span[0], part, sums, stage)]
    total = far(
        where, mid_partners, mids, sums[0], tops, interp_top[0], interp_mid[0], leaf_interpolant
    )
    return total.T


def solution(mesh):
    placed = (
        P(("leaf", "sub"), None),
        P(("leaf", "sub"), None),
        P(("leaf", "sub"), None),
        P(("leaf", "sub"), None, None),
        P(("leaf", "sub"), None),
        P(("leaf", "sub"), None, None),
        P(("leaf", "sub"), None),
        P(("leaf", "sub"), None),
        P("leaf", "sub", None),
        P("leaf", None),
    )
    return jax.shard_map(
        body, mesh=mesh, in_specs=placed, out_specs=P(("leaf", "sub"), None), check_vma=False
    )
```
